32 devices in a mesh: illum: 2 (over x), box: 16 (over z, y, core).
Axes of the slice: x: 2, y: 2, z: 4, core: 2. Of those that a mesh axis runs over, the one named last changes fastest.
Arguments:
- patterns: bfloat16 [2, 256, 128, 256], P(None, 'box', None, 'illum'), parts along dimension 3, may hold values from -6 to 6
- owner_block: int32 [4], replicated, may hold values from 0 to 31
- low_index: int32 [256, 48], P('box'), may hold values from 0 to 315
- low_mask: int32 [256, 48], P('box'), may hold values 0 or 1
- low_table: bfloat16 [2, 316, 128], replicated, may hold values from -2 to 2
- interp: bfloat16 [128, 512], replicated, may hold values from -0.5 to 0.5
- shift_angle: float32 [8, 512], replicated, may hold values from -3.140625 to 3.140625
- par_source: int32 [32, 16], replicated, may hold values from 0 to 31, as said below
- par_index: int32 [32, 16], replicated, may hold values from 0 to 315
- par_mask: int32 [32, 16], replicated, may hold values 0 or 1
- par_table: bfloat16 [2, 316, 512], replicated, may hold values from -1.5 to 1.5
Outputs:
- incoming: float32 [2, 256, 128, 256], P(None, 'box', None, 'illum'), parts along dimension 3
The draws below stay inside these ranges and needn't reach their ends.
There are 2 independent parts, one for each index of `illum`. The reference program is written for one: setup_inputs(seed, part) draws one part's arguments, and reference() takes and returns one part's arrays. A program takes and returns all parts, laid end to end along the dimension named above; an argument that names none is the same for every part. Nothing has to cross between parts.
Inputs may be any that keep to these rules, and one draw needn't show every extreme that they name: `par_source`: each parent's 16 slots name distinct parents other than itself.
All inputs are finite; a program needn't handle non-finite values. No bound on the sum of `low_mask` on one device may be relied on, other than what follows from the above.
Results may differ from the reference program's by a relative error of at most 0.0047.
Values may be sent and summed in bfloat16 or wider, within the bound.
A program may use at most 64 MiB of HBM per device.

```python
import jax
import jax.numpy as jnp
from jax import lax

K = 128
Q = 512
R = 128
BOX_DEV = 16
STEPS = 4
NTRANS = 316
PLIST = 16
BOXES = 256
BLOCKS = 32
PARENTS = 32
SRC = 48


def draw_par_source(key, part):
    row_keys = jax.random.split(jax.random.fold_in(key, 7), PARENTS)

    def one_row(row_key):
        rest = jax.random.permutation(row_key, PARENTS - 2).astype(jnp.int32) + 2
        return jnp.concatenate([jnp.ones((1,), jnp.int32), rest[:PLIST - 1]])
    offsets = jax.vmap(one_row)(row_keys)
    base = jnp.arange(PARENTS, dtype=jnp.int32)[:, None]
    return ((base + offsets) % PARENTS).astype(jnp.int32)


def place_ends(array, stream_key, least, top_value):
    longest = array.shape.index(max(array.shape))
    spots = []
    for shift in (0, 1):
        where = [jax.random.randint(jax.random.fold_in(stream_key, axis), (), 0, length) for axis, length in enumerate(array.shape)]
        where[longest] = (where[longest] + shift) % array.shape[longest]
        spots.append(tuple(where))
    return array.at[spots[0]].set(least).at[spots[1]].set(top_value)


def block_scale(rng, dims, pieces, smallest, high):
    def one(axis_at, blocks):
        draws = jax.random.uniform(jax.random.fold_in(jax.random.fold_in(rng, 6), axis_at), (blocks,), jnp.float32, smallest / len(pieces), high / len(pieces))
        return jnp.repeat(jnp.exp(draws), dims[axis_at] // blocks).reshape((-1,) + (1,) * (len(dims) - axis_at - 1))

    factor_of = one(*pieces[0])
    for cut in pieces[1:]:
        factor_of = factor_of * one(*cut)
    return factor_of


def gaussian(rng, shape, width, reach, pieces=(), kind=jnp.bfloat16):
    level = block_scale(rng, shape, pieces, -0.22, 0.18) if pieces else 1.0
    values = jax.random.normal(rng, shape, jnp.float32) * width * level
    return jnp.minimum(jnp.maximum(values, -reach), reach).astype(kind)


def setup_inputs(seed: int = 0, part: int = 0) -> dict:
    key_of = jax.random.split(jax.random.key(seed), 12)
    part_splits = jax.random.split(jax.random.fold_in(key_of[11], part), 12)
    return {
        "patterns": gaussian(part_splits[0], (2, BOXES, K, R), 1.0, 6.0, ((1, 16),)),
        "owner_block": place_ends(jax.random.randint(key_of[1], (STEPS,), 0, BLOCKS), jax.random.fold_in(key_of[1], 1), 0, BLOCKS - 1).astype(jnp.int32),
        "low_index": place_ends(jax.random.randint(key_of[2], (BOXES, SRC), 0, NTRANS), jax.random.fold_in(key_of[2], 1), 0, NTRANS - 1).astype(jnp.int32),
        "low_mask": place_ends((jax.random.randint(key_of[3], (BOXES, SRC), 0, 2) < 1).astype(jnp.int32), jax.random.fold_in(key_of[3], 1), 0, 1),
        "low_table": gaussian(key_of[4], (2, NTRANS, K), 0.15, 2.0),
        "interp": gaussian(key_of[5], (K, Q), K ** -0.5, 0.5),
        "shift_angle": jnp.clip(jax.random.uniform(key_of[6], (8, Q), jnp.float32, -3.140625, 3.140625), -3.140625, 3.140625),
        "par_source": draw_par_source(jax.random.fold_in(key_of[11], 71), part),
        "par_index": place_ends(jax.random.randint(key_of[8], (PARENTS, PLIST), 0, NTRANS), jax.random.fold_in(key_of[8], 1), 0, NTRANS - 1).astype(jnp.int32),
        "par_mask": place_ends((jax.random.randint(key_of[9], (PARENTS, PLIST), 0, 4) < 3).astype(jnp.int32), jax.random.fold_in(key_of[9], 1), 0, 1),
        "par_table": gaussian(key_of[10], (2, NTRANS, Q), 0.1, 1.5),
    }


def complex_apply(operator, sources):
    left_real = operator[0].astype(jnp.float32)
    left_imaginary = operator[1].astype(jnp.float32)
    right_real = sources[0].astype(jnp.float32)
    right_imaginary = sources[1].astype(jnp.float32)
    real_part = jnp.einsum('bjk,jkr->bkr', left_real, right_real) - jnp.einsum('bjk,jkr->bkr', left_imaginary, right_imaginary)
    imaginary = jnp.einsum('bjk,jkr->bkr', left_real, right_imaginary) + jnp.einsum('bjk,jkr->bkr', left_imaginary, right_real)
    return jnp.stack([real_part, imaginary])


def reference(patterns, owner_block, low_index, low_mask, low_table, interp, shift_angle, par_source, par_index, par_mask, par_table):
    boxes = patterns.shape[1]
    clusters = boxes // BOX_DEV
    blocks_each = BOX_DEV // 8
    far_ids = (owner_block[:, None] * 8 + jnp.arange(8, dtype=jnp.int32)[None, :]).reshape(-1).astype(jnp.int32)
    far_patterns = patterns[:, far_ids]
    cosine = jnp.cos(shift_angle)
    sine = jnp.sin(shift_angle)
    interp_wide = interp.astype(jnp.float32)

    def lift_cluster(cluster):
        child = lax.dynamic_slice_in_dim(patterns, cluster * BOX_DEV, BOX_DEV, 1).astype(jnp.float32)
        lifted = jnp.einsum('cbkr,kq->cbqr', child, interp_wide)
        lifted = lifted.reshape(2, blocks_each, 8, Q, R)
        real_part = jnp.sum(cosine[None, :, :, None] * lifted[0] - sine[None, :, :, None] * lifted[1], axis=1)
        imaginary = jnp.sum(cosine[None, :, :, None] * lifted[1] + sine[None, :, :, None] * lifted[0], axis=1)
        return jnp.stack([real_part, imaginary]).astype(jnp.bfloat16)

    lifted_all = lax.map(lift_cluster, jnp.arange(clusters, dtype=jnp.int32))
    parent_patterns = jnp.transpose(lifted_all, (1, 0, 2, 3, 4)).reshape(2, PARENTS, Q, R)

    def add_slot(slot, total):
        source = par_source[:, slot]
        which = par_index[:, slot]
        weight = par_mask[:, slot].astype(jnp.float32)
        picked = parent_patterns[:, source].astype(jnp.float32)
        operator = par_table[:, which].astype(jnp.float32) * weight[None, :, None]
        real_part = operator[0][:, :, None] * picked[0] - operator[1][:, :, None] * picked[1]
        imaginary = operator[0][:, :, None] * picked[1] + operator[1][:, :, None] * picked[0]
        return total + jnp.stack([real_part, imaginary])

    translated = lax.fori_loop(0, PLIST, add_slot, jnp.zeros((2, PARENTS, Q, R), jnp.float32)).astype(jnp.bfloat16)

    def finish_cluster(cluster):
        own = lax.dynamic_slice_in_dim(patterns, cluster * BOX_DEV, BOX_DEV, 1)
        sources = jnp.concatenate([own, far_patterns], axis=1)
        index = lax.dynamic_slice_in_dim(low_index, cluster * BOX_DEV, BOX_DEV, 0)
        keep = lax.dynamic_slice_in_dim(low_mask, cluster * BOX_DEV, BOX_DEV, 0).astype(jnp.float32)
        operator = low_table[:, index].astype(jnp.float32) * keep[None, :, :, None]
        near = complex_apply(jnp.transpose(operator, (0, 1, 2, 3)), sources)
        parents_here = lax.dynamic_slice_in_dim(translated, cluster * blocks_each, blocks_each, 1).astype(jnp.float32)
        wide = parents_here[:, :, None]
        real_part = cosine[None, :, :, None] * wide[0] + sine[None, :, :, None] * wide[1]
        imaginary = cosine[None, :, :, None] * wide[1] - sine[None, :, :, None] * wide[0]
        phased = jnp.stack([real_part, imaginary]).astype(jnp.bfloat16).reshape(2, BOX_DEV, Q, R)
        down = jnp.einsum('cbqr,kq->cbkr', phased.astype(jnp.float32), interp_wide)
        return near + down

    result = lax.map(finish_cluster, jnp.arange(clusters, dtype=jnp.int32))
    return jnp.transpose(result, (1, 0, 2, 3, 4)).reshape(2, boxes, K, R)
```

```python
import functools

import jax
import jax.numpy as jnp
from jax import lax
from jax.experimental import pallas as pl
from jax.experimental.pallas import tpu as pltpu
from jax.sharding import PartitionSpec as P

F32 = jnp.float32
BF16 = jnp.bfloat16
MESH = pl.DeviceIdType.MESH


def dot(left, right):
    return jnp.dot(left, right, preferred_element_type=F32)


def kernel(
    n,
    listed,
    chains,
    pitches,
    owner_ref,
    pat_ref,
    code_ref,
    table_ref,
    source_ref,
    index_ref,
    mask_ref,
    par_ref,
    interp_ref,
    angle_ref,
    out_ref,
    phase_ref,
    op,
    couple,
    parent,
    arrived,
    wide,
    result,
    result_send,
    returned,
    own,
    given,
    buf,
    landed,
    far,
    own_wide,
    acc,
    out_send,
    out_recv,
    back_send,
    back_recv,
    swap_send,
    swap_recv,
    rs_send,
    rs_recv,
    ag_send,
    ag_recv,
):
    me = lax.axis_index("box")
    core = me % 2
    boxes = pat_ref.shape[1]
    kdir, illums = pat_ref.shape[2], pat_ref.shape[3]
    groups8 = boxes // 8
    qdir = interp_ref.shape[1]
    qloc = qdir // n
    both_own = 2 * boxes
    span = kdir // 2 // chains
    order = list(range(1, n.bit_length() - 1))
    kpitch, bpitch, qpitch, ppitch = pitches

    barrier = pltpu.get_barrier_semaphore()

    def greet(i, carry):
        peer = lax.rem(me + i, n)
        pl.semaphore_signal(barrier, inc=1, device_id={"box": peer}, device_id_type=MESH)
        return carry

    lax.fori_loop(1, n, greet, 0)

    unroll = 8
    for part in range(2):
        for b in range(boxes):
            spot = b // 8 * 16 + part * 8 + b % 8
            own_wide[pl.ds(spot * kpitch, kdir), :] = pat_ref[part, b].astype(F32)

    def turn(t, carry):
        for u in range(unroll):
            k = t * unroll + u
            own[k] = own_wide[pl.ds(k, both_own, stride=kpitch), :].astype(BF16)
        return carry

    lax.fori_loop(0, kdir // unroll, turn, 0)

    def remote(src, dst, send, recv, bit):
        mine = me // (1 << bit) % 2
        return pltpu.make_async_remote_copy(
            src_ref=src,
            dst_ref=dst,
            send_sem=send,
            recv_sem=recv,
            device_id={"box": me + (1 - 2 * mine) * (1 << bit)},
            device_id_type=MESH,
        )

    def swap(chain):
        spots = own.at[pl.ds((1 - core) * (kdir // 2) + chain * span, span)]
        return remote(spots, given[chain], swap_send.at[chain], swap_recv.at[chain], 0)

    def place(chain, depth):
        low = core * (kdir // 2) + chain * span
        size = span
        for b in order[:depth]:
            size = size // 2
            low = low + me // (1 << b) % 2 * size
        return low, size

    def halving(chain, depth):
        bit = order[depth]
        low, size = place(chain, depth)
        size = size // 2
        give = low + (1 - me // (1 << bit) % 2) * size
        spot = chain * span + span - 2 * size
        return remote(
            buf.at[pl.ds(give, size)],
            landed.at[pl.ds(spot, size)],
            rs_send.at[chain, depth],
            rs_recv.at[chain, depth],
            bit,
        )

    def halve(chain, depth):
        halving(chain, depth).wait()
        low, size = place(chain, depth + 1)
        spot = chain * span + span - 2 * size
        target = far if depth + 1 == len(order) else buf
        target[pl.ds(low, size)] = buf[pl.ds(low, size)] + landed[pl.ds(spot, size)]
        if depth + 1 < len(order):
            halving(chain, depth + 1).start()
        else:
            doubling(chain, len(order)).start()

    def doubling(chain, depth):
        low, size = place(chain, depth)
        bit = order[depth - 1] if depth else 0
        spots = far.at[pl.ds(low, size)]
        return remote(spots, spots, ag_send.at[chain, depth], ag_recv.at[chain, depth], bit)

    def double(chain, depth):
        doubling(chain, depth).wait()
        doubling(chain, depth - 1).start()

    def merge(chain):
        swap(chain).wait()
        low, size = place(chain, 0)
        for step in range(listed):
            owner = owner_ref[step]
            device = owner // groups8
            rows = pl.ds(owner % groups8 * 16, 16)
            block = own[pl.ds(low, size), rows, :]
            theirs = given[chain][:, rows, :]
            block = jnp.where(device == me, block, jnp.where(device // 2 == me // 2, theirs, jnp.zeros_like(block)))
            buf[pl.ds(low, size), step * 16 : step * 16 + 16, :] = block
        halving(chain, 0).start()

    pl.semaphore_wait(barrier, n - 1)
    for chain in range(chains):
        swap(chain).start()
    phase_ref[:, :8] = jnp.cos(angle_ref[...]).T
    phase_ref[:, 8:] = jnp.sin(angle_ref[...]).T
    for chain in range(chains):
        merge(chain)

    def out_copy(i, parent_at):
        peer = lax.rem(me + i, n)
        return pltpu.make_async_remote_copy(
            src_ref=parent.at[pl.ds(2 * parent_at, 2), pl.ds(pl.multiple_of(peer * qloc, qloc), qloc), :],
            dst_ref=arrived.at[me, pl.ds(2 * parent_at, 2)],
            send_sem=out_send.at[parent_at, i],
            recv_sem=out_recv.at[parent_at, i],
            device_id={"box": peer},
            device_id_type=MESH,
        )

    tile = 256
    for parent_at in range(groups8):

        def lift(t, carry, parent_at=parent_at):
            at = pl.multiple_of(t * tile, tile)
            left = interp_ref[:, pl.ds(at, tile)].T
            real = jnp.zeros((tile, illums), F32)
            imag = jnp.zeros((tile, illums), F32)
            for child in range(8):
                b = parent_at * 8 + child
                both = dot(left, jnp.concatenate([pat_ref[0, b], pat_ref[1, b]], axis=1))
                cosine = phase_ref[pl.ds(at, tile), child : child + 1]
                sine = phase_ref[pl.ds(at, tile), 8 + child : 9 + child]
                re, im = both[:, :illums], both[:, illums:]
                real = real + (cosine * re - sine * im)
                imag = imag + (cosine * im + sine * re)
            parent[2 * parent_at, pl.ds(at, tile), :] = real.astype(BF16)
            parent[2 * parent_at + 1, pl.ds(at, tile), :] = imag.astype(BF16)
            return carry

        lax.fori_loop(0, qdir // tile, lift, 0)

        def start_out(i, carry, parent_at=parent_at):
            out_copy(i, parent_at).start()
            return carry

        lax.fori_loop(1, n, start_out, 0)

    parents = n * groups8
    parents2 = 2 * parents

    lanes = lax.broadcasted_iota(jnp.int32, (parents, parents), 1)
    code = jnp.zeros((parents, parents), jnp.int32)
    slot_code = jnp.where(mask_ref[...] > 0, index_ref[...] + 1, 0).T
    slot_source = source_ref[...].T
    for j in range(source_ref.shape[0]):
        code = code + jnp.where(slot_source[:, j : j + 1] == lanes, slot_code[:, j : j + 1], 0)
    code = jnp.concatenate([code, code], axis=1) - 1
    each = max(1, 256 // parents2)
    kinds = lax.broadcasted_iota(jnp.int32, (par_ref.shape[1], each * parents2), 0)
    first = lax.broadcasted_iota(jnp.int32, (qloc, parents2), 1) < parents
    for p in range(0, parents, each):
        row = jnp.concatenate([code[p + u : p + u + 1] for u in range(each)], axis=1)
        hot = jnp.where(kinds == row, 1.0, 0.0).astype(BF16)
        got = dot(par_ref[...], hot)
        for u in range(each):
            real = got[:qloc, u * parents2 : (u + 1) * parents2]
            imag = got[qloc:, u * parents2 : (u + 1) * parents2]
            couple[pl.ds(p + u, qloc, stride=ppitch), :] = jnp.where(first, real, -imag)
            couple[pl.ds(parents + p + u, qloc, stride=ppitch), :] = jnp.where(first, imag, real)

    for chain in range(chains):
        halve(chain, 0)

    width = code_ref.shape[1]
    low_kinds = lax.broadcasted_iota(jnp.int32, (table_ref.shape[1], 2 * width), 0)
    low_first = lax.broadcasted_iota(jnp.int32, (kdir, width), 1) // 8 % 2 == 0
    for b in range(0, boxes, 2):
        row = jnp.concatenate([code_ref[b : b + 1], code_ref[b + 1 : b + 2]], axis=1)
        hot = jnp.where(low_kinds == row, 1.0, 0.0).astype(BF16)
        got = dot(table_ref[...], hot)
        for u in range(2):
            real = got[:kdir, u * width : (u + 1) * width]
            imag = got[kdir:, u * width : (u + 1) * width]
            op[pl.ds(b + u, kdir, stride=bpitch), :] = jnp.where(low_first, real, -imag)
            op[pl.ds(boxes + b + u, kdir, stride=bpitch), :] = jnp.where(low_first, imag, real)

    for depth in range(1, len(order)):
        for chain in range(chains):
            halve(chain, depth)
    for depth in range(len(order), 1, -1):
        for chain in range(chains):
            double(chain, depth)

    def widen(source, value):
        for part in range(2):
            for p in range(groups8):
                s = (part * n + source) * groups8 + p
                at = pl.multiple_of(s * qpitch, 8)
                wide[pl.ds(at, qloc), :] = value(p * 2 + part).astype(F32)

    widen(me, lambda c: parent[c, pl.ds(pl.multiple_of(me * qloc, qloc), qloc), :])

    def take(i, carry):
        for parent_at in range(groups8):
            out_copy(i, parent_at).wait()
        source = lax.rem(me - i + n, n)
        widen(source, lambda c: arrived[source, c])
        return carry

    lax.fori_loop(1, n, take, 0)

    def translate(t, carry):
        for u in range(unroll):
            q = t * unroll + u
            sources = wide[pl.ds(q, parents2, stride=qpitch), :].astype(BF16)
            result[pl.ds(q, parents2, stride=qpitch), :] = dot(
                couple[pl.ds(pl.multiple_of(q * ppitch, 8), parents2), :].astype(BF16), sources
            )
        return carry

    lax.fori_loop(0, qloc // unroll, translate, 0)
    for s in range(parents2):
        result_send[s // parents, s % parents] = result[pl.ds(s * qpitch, qloc), :].astype(BF16)

    def back_copy(i):
        peer = lax.rem(me + i, n)
        return pltpu.make_async_remote_copy(
            src_ref=result_send.at[:, pl.ds(peer * groups8, groups8)],
            dst_ref=returned.at[:, :, pl.ds(pl.multiple_of(me * qloc, qloc), qloc), :],
            send_sem=back_send.at[i],
            recv_sem=back_recv.at[i],
            device_id={"box": peer},
            device_id_type=MESH,
        )

    def start_back(i, carry):
        back_copy(i).start()
        return carry

    lax.fori_loop(1, n, start_back, 0)
    returned[:, :, pl.ds(pl.multiple_of(me * qloc, qloc), qloc), :] = result_send[:, pl.ds(me * groups8, groups8)]

    def near(at):
        def one(t, carry):
            sums = []
            for u in range(unroll):
                k = at + t * unroll + u
                operator = op[pl.ds(pl.multiple_of(k * bpitch, 8), both_own), :].astype(BF16)
                sources = jnp.concatenate([own[k], far[k]], axis=0)
                sums.append(dot(operator[:, : both_own + 16 * listed], sources))
            for u in range(unroll):
                acc[pl.ds(at + t * unroll + u, both_own, stride=kpitch), :] = sums[u]
            return carry

        lax.fori_loop(0, span // unroll, one, 0)

    for chain in range(chains):
        double(chain, 1)
        near(core * (kdir // 2) + chain * span)

    for chain in range(chains):
        doubling(chain, 0).wait()
        near((1 - core) * (kdir // 2) + chain * span)

    def land(i, carry):
        back_copy(i).wait()
        return carry

    lax.fori_loop(1, n, land, 0)

    for parent_at in range(groups8):
        for child in range(8):
            b = parent_at * 8 + child
            re = returned[0, parent_at].astype(F32)
            im = returned[1, parent_at].astype(F32)
            cosine = phase_ref[:, child : child + 1]
            sine = phase_ref[:, 8 + child : 9 + child]
            real = (cosine * re + sine * im).astype(BF16)
            imag = (cosine * im - sine * re).astype(BF16)
            both = dot(interp_ref[...], jnp.concatenate([real, imag], axis=1))
            out_ref[pl.ds(b * kdir, kdir), :] = both[:, :illums] + acc[pl.ds(b * kpitch, kdir), :]
            out_ref[pl.ds((boxes + b) * kdir, kdir), :] = (
                both[:, illums:] + acc[pl.ds((boxes + b) * kpitch, kdir), :]
            )


def shards(
    patterns,
    owner_block,
    low_index,
    low_mask,
    low_table,
    interp,
    shift_angle,
    par_source,
    par_index,
    par_mask,
    par_table,
):
    boxes, kdir, illums = patterns.shape[1:]
    groups8 = boxes // 8
    qdir = interp.shape[1]
    n = lax.axis_size("box")
    listed = owner_block.shape[0]
    parents = par_source.shape[0]
    qloc = qdir // n
    sources = low_index.shape[1]
    chains = 4

    code = jnp.where(low_mask > 0, low_index, -1)
    code = jnp.repeat(code.reshape(boxes, sources // 8, 1, 8), 2, axis=2).reshape(boxes, 2 * sources)
    code = jnp.pad(code, ((0, 0), (0, -2 * sources % 128)), constant_values=-1)
    low = jnp.transpose(low_table, (0, 2, 1)).reshape(2 * kdir, -1)
    start = lax.axis_index("box") * qloc
    table = lax.dynamic_slice_in_dim(par_table, start, qloc, 2)
    table = jnp.transpose(table, (0, 2, 1)).reshape(2 * qloc, -1)

    pitches = (kdir + 8, 2 * boxes + 8, qloc + 8, 2 * parents + 8)
    kpitch, bpitch, qpitch, ppitch = pitches
    vmem = pl.BlockSpec(memory_space=pltpu.VMEM)
    smem = pl.BlockSpec(memory_space=pltpu.SMEM)
    stages = n.bit_length() - 1
    dma = pltpu.SemaphoreType.DMA
    return pl.pallas_call(
        functools.partial(kernel, n, listed, chains, pitches),
        out_shape=jax.ShapeDtypeStruct((2 * boxes * kdir, illums), F32),
        in_specs=[smem] + [vmem] * 9,
        out_specs=vmem,
        scratch_shapes=[
            pltpu.VMEM((qdir, 16), F32),
            pltpu.VMEM((kdir * bpitch, code.shape[1]), F32),
            pltpu.VMEM((qloc * ppitch, 2 * parents), F32),
            pltpu.VMEM((2 * groups8, qdir, illums), BF16),
            pltpu.VMEM((n, 2 * groups8, qloc, illums), BF16),
            pltpu.VMEM((2 * parents * qpitch, illums), F32),
            pltpu.VMEM((2 * parents * qpitch, illums), F32),
            pltpu.VMEM((2, parents, qloc, illums), BF16),
            pltpu.VMEM((2, groups8, qdir, illums), BF16),
            pltpu.VMEM((kdir, 2 * boxes, illums), BF16),
            [pltpu.VMEM((kdir // 2 // chains, 2 * boxes, illums), BF16) for _ in range(chains)],
            pltpu.VMEM((kdir, 16 * listed, illums), BF16),
            pltpu.VMEM((kdir // 2, 16 * listed, illums), BF16),
            pltpu.VMEM((kdir, 16 * listed, illums), BF16),
            pltpu.VMEM((2 * boxes * kpitch, illums), F32),
            pltpu.VMEM((2 * boxes * kpitch, illums), F32),
            dma((groups8, n)),
            dma((groups8, n)),
            dma((n,)),
            dma((n,)),
            dma((chains,)),
            dma((chains,)),
            dma((chains, stages)),
            dma((chains, stages)),
            dma((chains, stages)),
            dma((chains, stages)),
        ],
        compiler_params=pltpu.CompilerParams(
            collective_id=0, has_side_effects=True, vmem_limit_bytes=56 * 1024 * 1024
        ),
    )(
        owner_block,
        patterns,
        code,
        low,
        par_source.T,
        par_index.T,
        par_mask.T,
        table,
        interp,
        shift_angle,
    ).reshape(2, boxes, kdir, illums)


def solution(mesh):
    placed = (
        P(None, "box", None, "illum"),
        P(),
        P("box", None),
        P("box", None),
        P(),
        P(),
        P(),
        P(),
        P(),
        P(),
        P(),
    )
    return jax.shard_map(
        shards, mesh=mesh, in_specs=placed, out_specs=P(None, "box", None, "illum"), check_vma=False
    )
```

```python
import functools

import jax
import jax.numpy as jnp
from jax import lax
from jax.experimental import pallas as pl
from jax.experimental.pallas import tpu as pltpu
from jax.sharding import PartitionSpec as P

F32 = jnp.float32
BF16 = jnp.bfloat16
MESH = pl.DeviceIdType.MESH


def dot(left, right):
    return jnp.dot(left, right, preferred_element_type=F32)


def dot_rows(left, right):
    return lax.dot_general(left, right, (((0,), (0,)), ((), ())), preferred_element_type=F32)


def kernel(
    n,
    listed,
    chains,
    pitches,
    owner_ref,
    pat_ref,
    low_index_ref,
    low_mask_ref,
    table_ref,
    source_ref,
    index_ref,
    mask_ref,
    par_ref,
    interp_ref,
    angle_ref,
    out_ref,
    phase_ref,
    op,
    couple,
    parent,
    arrived,
    wide,
    result,
    result_send,
    returned,
    own,
    given,
    buf,
    landed,
    far,
    own_wide,
    acc,
    out_send,
    out_recv,
    back_send,
    back_recv,
    swap_send,
    swap_recv,
    rs_send,
    rs_recv,
    ag_send,
    ag_recv,
):
    me = lax.axis_index("box")
    core = me % 2
    boxes = pat_ref.shape[1]
    kdir, illums = pat_ref.shape[2], pat_ref.shape[3]
    groups8 = boxes // 8
    qdir = interp_ref.shape[1]
    qloc = qdir // n
    both_own = 2 * boxes
    span = kdir // 2 // chains
    bits = list(range(1, n.bit_length() - 1))
    orders = [bits for _ in range(chains)]
    deep = len(bits) - 1
    kpitch, bpitch, qpitch, ppitch = pitches

    barrier = pltpu.get_barrier_semaphore()

    def greet(i, carry):
        peer = lax.rem(me + i, n)
        pl.semaphore_signal(barrier, inc=1, device_id={"box": peer}, device_id_type=MESH)
        return carry

    lax.fori_loop(1, n, greet, 0)

    unroll = 8
    for part in range(2):
        for b in range(boxes):
            spot = b // 8 * 16 + part * 8 + b % 8
            own_wide[pl.ds(spot * kpitch, kdir), :] = pat_ref[part, b].astype(F32)

    def turn(t, carry):
        for u in range(unroll):
            k = t * unroll + u
            own[k] = own_wide[pl.ds(k, both_own, stride=kpitch), :].astype(BF16)
        return carry

    lax.fori_loop(0, kdir // unroll, turn, 0)

    def remote(src, dst, send, recv, bit):
        mine = me // (1 << bit) % 2
        return pltpu.make_async_remote_copy(
            src_ref=src,
            dst_ref=dst,
            send_sem=send,
            recv_sem=recv,
            device_id={"box": me + (1 - 2 * mine) * (1 << bit)},
            device_id_type=MESH,
        )

    def swap(chain):
        spots = own.at[pl.ds((1 - core) * (kdir // 2) + chain * span, span)]
        return remote(spots, given[chain], swap_send.at[chain], swap_recv.at[chain], 0)

    def place(chain, depth):
        low = core * (kdir // 2) + chain * span
        size = span
        for b in orders[chain][:depth]:
            size = size // 2
            low = low + me // (1 << b) % 2 * size
        return low, size

    def reduction(chain, depth):
        bit = orders[chain][depth]
        low, size = place(chain, depth)
        if depth < deep:
            size = size // 2
            low = low + (1 - me // (1 << bit) % 2) * size
        spot = chain * span + span - (span >> depth)
        return remote(
            buf.at[pl.ds(low, size)],
            landed.at[pl.ds(spot, size)],
            rs_send.at[chain, depth],
            rs_recv.at[chain, depth],
            bit,
        )

    def reduce(chain, depth):
        reduction(chain, depth).wait()
        low, size = place(chain, min(depth + 1, deep))
        spot = chain * span + span - (span >> depth)
        target = far if depth == deep else buf
        target[pl.ds(low, size)] = buf[pl.ds(low, size)] + landed[pl.ds(spot, size)]
        if depth < deep:
            reduction(chain, depth + 1).start()
        else:
            doubling(chain, deep).start()

    def doubling(chain, depth):
        low, size = place(chain, depth)
        bit = orders[chain][depth - 1] if depth else 0
        spots = far.at[pl.ds(low, size)]
        return remote(spots, spots, ag_send.at[chain, depth], ag_recv.at[chain, depth], bit)

    def double(chain, depth):
        doubling(chain, depth).wait()
        doubling(chain, depth - 1).start()

    def merge(chain):
        swap(chain).wait()
        low, size = place(chain, 0)
        for step in range(listed):
            owner = owner_ref[step]
            device = owner // groups8
            rows = pl.ds(owner % groups8 * 16, 16)
            block = own[pl.ds(low, size), rows, :]
            theirs = given[chain][:, rows, :]
            block = jnp.where(device == me, block, jnp.where(device // 2 == me // 2, theirs, jnp.zeros_like(block)))
            buf[pl.ds(low, size), step * 16 : step * 16 + 16, :] = block
        reduction(chain, 0).start()

    phase_ref[:, :8] = jnp.cos(angle_ref[...]).T
    phase_ref[:, 8:] = jnp.sin(angle_ref[...]).T

    def out_copy(i, parent_at):
        peer = lax.rem(me + i, n)
        return pltpu.make_async_remote_copy(
            src_ref=parent.at[pl.ds(2 * parent_at, 2), pl.ds(pl.multiple_of(peer * qloc, qloc), qloc), :],
            dst_ref=arrived.at[me, pl.ds(2 * parent_at, 2)],
            send_sem=out_send.at[parent_at],
            recv_sem=out_recv.at[parent_at],
            device_id={"box": peer},
            device_id_type=MESH,
        )

    tile = 256
    def lift_parent(parent_at):
        def lift(t, carry):
            at = pl.multiple_of(t * tile, tile)
            left = interp_ref[:, pl.ds(at, tile)].T
            real = jnp.zeros((tile, illums), F32)
            imag = jnp.zeros((tile, illums), F32)
            for child in range(8):
                b = parent_at * 8 + child
                both = dot(left, jnp.concatenate([pat_ref[0, b], pat_ref[1, b]], axis=1))
                cosine = phase_ref[pl.ds(at, tile), child : child + 1]
                sine = phase_ref[pl.ds(at, tile), 8 + child : 9 + child]
                re, im = both[:, :illums], both[:, illums:]
                real = real + (cosine * re - sine * im)
                imag = imag + (cosine * im + sine * re)
            parent[2 * parent_at, pl.ds(at, tile), :] = real.astype(BF16)
            parent[2 * parent_at + 1, pl.ds(at, tile), :] = imag.astype(BF16)
            return carry

        lax.fori_loop(0, qdir // tile, lift, 0)

    def send_out(parent_at, low, high):
        def start_out(i, carry):
            out_copy(i, parent_at).start()
            return carry

        lax.fori_loop(low, high, start_out, 0)

    parents = n * groups8
    parents2 = 2 * parents

    def build_couple():
        lanes = lax.broadcasted_iota(jnp.int32, (parents, parents), 1)
        code = jnp.zeros((parents, parents), jnp.int32)
        slot_code = jnp.where(mask_ref[...] > 0, index_ref[...] + 1, 0).T
        slot_source = source_ref[...].T
        for j in range(source_ref.shape[0]):
            code = code + jnp.where(slot_source[:, j : j + 1] == lanes, slot_code[:, j : j + 1], 0)
        code = jnp.concatenate([code, code], axis=1) - 1
        each = max(1, 256 // parents2)
        kinds = lax.broadcasted_iota(jnp.int32, (par_ref.shape[1], each * parents2), 0)
        first = lax.broadcasted_iota(jnp.int32, (qloc, parents2), 1) < parents
        for p in range(0, parents, each):
            row = jnp.concatenate([code[p + u : p + u + 1] for u in range(each)], axis=1)
            hot = jnp.where(kinds == row, 1.0, 0.0).astype(BF16)
            got = [dot_rows(par_ref[part], hot) for part in range(2)]
            for u in range(each):
                real = got[0][:, u * parents2 : (u + 1) * parents2]
                imag = got[1][:, u * parents2 : (u + 1) * parents2]
                couple[pl.ds(p + u, qloc, stride=ppitch), :] = jnp.where(first, real, -imag)
                couple[pl.ds(parents + p + u, qloc, stride=ppitch), :] = jnp.where(first, imag, real)

    def build_op():
        sources = low_index_ref.shape[1]
        width = 2 * sources + -2 * sources % 128
        wanted = jnp.where(low_mask_ref[...] > 0, low_index_ref[...] + 1, 0)
        column = lax.broadcasted_iota(jnp.int32, (sources, width), 1)
        spread = lax.broadcasted_iota(jnp.int32, (sources, width), 0) == column // 16 * 8 + column % 8
        spread = jnp.where(spread, 1.0, 0.0).astype(BF16)
        high = dot((wanted // 16).astype(F32).astype(BF16), spread)
        rest = dot((wanted % 16).astype(F32).astype(BF16), spread)
        code = (16 * high + rest).astype(jnp.int32) - 1
        low_kinds = lax.broadcasted_iota(jnp.int32, (table_ref.shape[1], 2 * width), 0)
        low_first = lax.broadcasted_iota(jnp.int32, (kdir, width), 1) // 8 % 2 == 0
        for b in range(0, boxes, 2):
            row = jnp.concatenate([code[b : b + 1], code[b + 1 : b + 2]], axis=1)
            hot = jnp.where(low_kinds == row, 1.0, 0.0).astype(BF16)
            got = [dot_rows(table_ref[part], hot) for part in range(2)]
            for u in range(2):
                real = got[0][:, u * width : (u + 1) * width]
                imag = got[1][:, u * width : (u + 1) * width]
                op[pl.ds(b + u, kdir, stride=bpitch), :] = jnp.where(low_first, real, -imag)
                op[pl.ds(boxes + b + u, kdir, stride=bpitch), :] = jnp.where(low_first, imag, real)

    def widen(source, value):
        for part in range(2):
            for p in range(groups8):
                s = (part * n + source) * groups8 + p
                at = pl.multiple_of(s * qpitch, 8)
                wide[pl.ds(at, qloc), :] = value(p * 2 + part).astype(F32)

    def back_copy(i):
        peer = lax.rem(me + i, n)
        return pltpu.make_async_remote_copy(
            src_ref=result_send.at[:, pl.ds(peer * groups8, groups8)],
            dst_ref=returned.at[:, :, pl.ds(pl.multiple_of(me * qloc, qloc), qloc), :],
            send_sem=back_send.at[0],
            recv_sem=back_recv.at[0],
            device_id={"box": peer},
            device_id_type=MESH,
        )

    def exchange():
        widen(me, lambda c: parent[c, pl.ds(pl.multiple_of(me * qloc, qloc), qloc), :])

        for parent_at in range(groups8):
            whole = arrived.at[pl.ds(0, n - 1), pl.ds(2 * parent_at, 2)]
            remote(whole, whole, out_send.at[parent_at], out_recv.at[parent_at], 0).wait()

        def take(i, carry):
            source = lax.rem(me - i + n, n)
            widen(source, lambda c: arrived[source, c])
            return carry

        lax.fori_loop(1, n, take, 0)

        def translate(t, carry):
            for u in range(unroll):
                q = t * unroll + u
                sources = wide[pl.ds(q, parents2, stride=qpitch), :].astype(BF16)
                result[pl.ds(q, parents2, stride=qpitch), :] = dot(
                    couple[pl.ds(pl.multiple_of(q * ppitch, 8), parents2), :].astype(BF16), sources
                )
            return carry

        lax.fori_loop(0, qloc // unroll, translate, 0)
        for s in range(parents2):
            result_send[s // parents, s % parents] = result[pl.ds(s * qpitch, qloc), :].astype(BF16)

    def send_back():
        def start_back(i, carry):
            back_copy(i).start()
            return carry

        lax.fori_loop(1, n, start_back, 0)
        returned[:, :, pl.ds(pl.multiple_of(me * qloc, qloc), qloc), :] = result_send[:, pl.ds(me * groups8, groups8)]

    def near(at):
        def one(t, carry):
            sums = []
            for u in range(unroll):
                k = at + t * unroll + u
                operator = op[pl.ds(pl.multiple_of(k * bpitch, 8), both_own), :].astype(BF16)
                sources = jnp.concatenate([own[k], far[k]], axis=0)
                sums.append(dot(operator[:, : both_own + 16 * listed], sources))
            for u in range(unroll):
                acc[pl.ds(at + t * unroll + u, both_own, stride=kpitch), :] = sums[u]
            return carry

        lax.fori_loop(0, span // unroll, one, 0)

    def finish():
        whole = returned.at[:, :, pl.ds(0, (n - 1) * qloc), :]
        remote(whole, whole, back_send.at[0], back_recv.at[0], 0).wait()
        for parent_at in range(groups8):
            for child in range(8):
                b = parent_at * 8 + child
                re = returned[0, parent_at].astype(F32)
                im = returned[1, parent_at].astype(F32)
                cosine = phase_ref[:, child : child + 1]
                sine = phase_ref[:, 8 + child : 9 + child]
                real = (cosine * re + sine * im).astype(BF16)
                imag = (cosine * im - sine * re).astype(BF16)
                both = dot(interp_ref[...], jnp.concatenate([real, imag], axis=1))
                out_ref[pl.ds(b * kdir, kdir), :] = both[:, :illums] + acc[pl.ds(b * kpitch, kdir), :]
                out_ref[pl.ds((boxes + b) * kdir, kdir), :] = (
                    both[:, illums:] + acc[pl.ds((boxes + b) * kpitch, kdir), :]
                )

    last_step = 2 * deep + 1

    def far_step(chain, step):
        if step <= deep:
            reduce(chain, step)
        elif step < last_step:
            double(chain, last_step - step)
            if step == last_step - 1:
                near(core * (kdir // 2) + chain * span)
        else:
            doubling(chain, 0).wait()
            near((1 - core) * (kdir // 2) + chain * span)

    def far_slot(slot):
        for chain in range(chains):
            if 0 <= slot - chain <= last_step:
                far_step(chain, slot - chain)

    slots = chains + last_step

    lift_parent(0)
    lift_parent(1)
    build_couple()
    build_op()
    pl.semaphore_wait(barrier, n - 1)
    for chain in range(chains):
        swap(chain).start()

    send_out(0, 1, n)
    for chain in range(chains):
        merge(chain)
    send_out(1, 1, n)
    for slot in range(5): far_slot(slot)
    exchange()
    send_back()
    for slot in range(5, slots): far_slot(slot)
    finish()


def shards(
    patterns,
    owner_block,
    low_index,
    low_mask,
    low_table,
    interp,
    shift_angle,
    par_source,
    par_index,
    par_mask,
    par_table,
):
    boxes, kdir, illums = patterns.shape[1:]
    groups8 = boxes // 8
    qdir = interp.shape[1]
    n = lax.axis_size("box")
    listed = owner_block.shape[0]
    parents = par_source.shape[0]
    qloc = qdir // n
    sources = low_index.shape[1]
    chains = 4

    start = lax.axis_index("box") * qloc
    table = lax.dynamic_slice_in_dim(par_table, start, qloc, 2)

    pitches = (kdir + 8, 2 * boxes + 8, qloc + 8, 2 * parents + 8)
    kpitch, bpitch, qpitch, ppitch = pitches
    vmem = pl.BlockSpec(memory_space=pltpu.VMEM)
    smem = pl.BlockSpec(memory_space=pltpu.SMEM)
    stages = n.bit_length() - 1
    dma = pltpu.SemaphoreType.DMA
    return pl.pallas_call(
        functools.partial(kernel, n, listed, chains, pitches),
        out_shape=jax.ShapeDtypeStruct((2 * boxes * kdir, illums), F32),
        in_specs=[smem] + [vmem] * 10,
        out_specs=vmem,
        scratch_shapes=[
            pltpu.VMEM((qdir, 16), F32),
            pltpu.VMEM((kdir * bpitch, 2 * sources + -2 * sources % 128), F32),
            pltpu.VMEM((qloc * ppitch, 2 * parents), F32),
            pltpu.VMEM((2 * groups8, qdir, illums), BF16),
            pltpu.VMEM((n, 2 * groups8, qloc, illums), BF16),
            pltpu.VMEM((2 * parents * qpitch, illums), F32),
            pltpu.VMEM((2 * parents * qpitch, illums), F32),
            pltpu.VMEM((2, parents, qloc, illums), BF16),
            pltpu.VMEM((2, groups8, qdir, illums), BF16),
            pltpu.VMEM((kdir, 2 * boxes, illums), BF16),
            [pltpu.VMEM((kdir // 2 // chains, 2 * boxes, illums), BF16) for _ in range(chains)],
            pltpu.VMEM((kdir, 16 * listed, illums), BF16),
            pltpu.VMEM((kdir // 2, 16 * listed, illums), BF16),
            pltpu.VMEM((kdir, 16 * listed, illums), BF16),
            pltpu.VMEM((2 * boxes * kpitch, illums), F32),
            pltpu.VMEM((2 * boxes * kpitch, illums), F32),
            dma((groups8,)),
            dma((groups8,)),
            dma((1,)),
            dma((1,)),
            dma((chains,)),
            dma((chains,)),
            dma((chains, stages - 1)),
            dma((chains, stages - 1)),
            dma((chains, stages - 1)),
            dma((chains, stages - 1)),
        ],
        compiler_params=pltpu.CompilerParams(
            collective_id=0, has_side_effects=True, vmem_limit_bytes=56 * 1024 * 1024
        ),
    )(
        owner_block,
        patterns,
        low_index,
        low_mask,
        low_table,
        par_source.T,
        par_index.T,
        par_mask.T,
        table,
        interp,
        shift_angle,
    ).reshape(2, boxes, kdir, illums)


def solution(mesh):
    placed = (
        P(None, "box", None, "illum"),
        P(),
        P("box", None),
        P("box", None),
        P(),
        P(),
        P(),
        P(),
        P(),
        P(),
        P(),
    )
    return jax.shard_map(
        shards, mesh=mesh, in_specs=placed, out_specs=P(None, "box", None, "illum"), check_vma=False
    )
```

```python
import functools

import jax
import jax.numpy as jnp
from jax import lax
from jax.experimental import pallas as pl
from jax.experimental.pallas import tpu as pltpu
from jax.sharding import PartitionSpec as P

F32 = jnp.float32
BF16 = jnp.bfloat16
MESH = pl.DeviceIdType.MESH


def dot(left, right):
    return jnp.dot(left, right, preferred_element_type=F32)


def dot_rows(left, right):
    return lax.dot_general(left, right, (((0,), (0,)), ((), ())), preferred_element_type=F32)


def kernel(
    n,
    listed,
    chains,
    pitches,
    owner_ref,
    pat_ref,
    low_index_ref,
    low_mask_ref,
    table_ref,
    source_ref,
    index_ref,
    mask_ref,
    par_ref,
    interp_ref,
    angle_ref,
    out_ref,
    phase_ref,
    op,
    couple,
    parent,
    arrived,
    wide,
    result,
    result_send,
    returned,
    own,
    given,
    buf,
    landed,
    far,
    own_wide,
    acc,
    out_send,
    out_recv,
    back_send,
    back_recv,
    swap_send,
    swap_recv,
    rs_send,
    rs_recv,
    ag_send,
    ag_recv,
):
    me = lax.axis_index("box")
    core = me % 2
    boxes = pat_ref.shape[1]
    kdir, illums = pat_ref.shape[2], pat_ref.shape[3]
    groups8 = boxes // 8
    qdir = interp_ref.shape[1]
    qloc = qdir // n
    both_own = 2 * boxes
    span = kdir // 2 // chains
    bits = list(range(1, n.bit_length() - 1))
    orders = [bits for _ in range(chains)]
    deep = len(bits) - 1
    kpitch, bpitch, qpitch, ppitch = pitches

    barrier = pltpu.get_barrier_semaphore()

    def greet(i, carry):
        peer = lax.rem(me + i, n)
        pl.semaphore_signal(barrier, inc=1, device_id={"box": peer}, device_id_type=MESH)
        return carry

    lax.fori_loop(1, n, greet, 0)

    unroll = 8
    for part in range(2):
        for b in range(boxes):
            spot = b // 8 * 16 + part * 8 + b % 8
            own_wide[pl.ds(spot * kpitch, kdir), :] = pat_ref[part, b].astype(F32)

    def turn(t, carry):
        for u in range(unroll):
            k = t * unroll + u
            own[k] = own_wide[pl.ds(k, both_own, stride=kpitch), :].astype(BF16)
        return carry

    lax.fori_loop(0, kdir // unroll, turn, 0)

    def remote(src, dst, send, recv, bit):
        mine = me // (1 << bit) % 2
        return pltpu.make_async_remote_copy(
            src_ref=src,
            dst_ref=dst,
            send_sem=send,
            recv_sem=recv,
            device_id={"box": me + (1 - 2 * mine) * (1 << bit)},
            device_id_type=MESH,
        )

    def swap(chain):
        spots = own.at[pl.ds((1 - core) * (kdir // 2) + chain * span, span)]
        return remote(spots, given[chain], swap_send.at[chain], swap_recv.at[chain], 0)

    def place(chain, depth):
        low = core * (kdir // 2) + chain * span
        size = span
        for b in orders[chain][:depth]:
            size = size // 2
            low = low + me // (1 << b) % 2 * size
        return low, size

    def reduction(chain, depth):
        bit = orders[chain][depth]
        low, size = place(chain, depth)
        if depth < deep:
            size = size // 2
            low = low + (1 - me // (1 << bit) % 2) * size
        spot = chain * span + span - (span >> depth)
        return remote(
            buf.at[pl.ds(low, size)],
            landed.at[pl.ds(spot, size)],
            rs_send.at[chain, depth],
            rs_recv.at[chain, depth],
            bit,
        )

    def reduce(chain, depth):
        reduction(chain, depth).wait()
        low, size = place(chain, min(depth + 1, deep))
        spot = chain * span + span - (span >> depth)
        target = far if depth == deep else buf
        target[pl.ds(low, size)] = buf[pl.ds(low, size)] + landed[pl.ds(spot, size)]
        if depth < deep:
            reduction(chain, depth + 1).start()
        else:
            doubling(chain, deep).start()

    def doubling(chain, depth):
        low, size = place(chain, depth)
        bit = orders[chain][depth - 1] if depth else 0
        spots = far.at[pl.ds(low, size)]
        return remote(spots, spots, ag_send.at[chain, depth], ag_recv.at[chain, depth], bit)

    def double(chain, depth):
        doubling(chain, depth).wait()
        doubling(chain, depth - 1).start()

    def merge(chain):
        swap(chain).wait()
        low, size = place(chain, 0)
        for step in range(listed):
            owner = owner_ref[step]
            device = owner // groups8
            rows = pl.ds(owner % groups8 * 16, 16)
            block = own[pl.ds(low, size), rows, :]
            theirs = given[chain][:, rows, :]
            block = jnp.where(device == me, block, jnp.where(device // 2 == me // 2, theirs, jnp.zeros_like(block)))
            buf[pl.ds(low, size), step * 16 : step * 16 + 16, :] = block
        reduction(chain, 0).start()

    phase_ref[:, :8] = jnp.cos(angle_ref[...]).T
    phase_ref[:, 8:] = jnp.sin(angle_ref[...]).T

    def out_copy(i, parent_at):
        peer = lax.rem(me + i, n)
        return pltpu.make_async_remote_copy(
            src_ref=parent.at[pl.ds(2 * parent_at, 2), pl.ds(pl.multiple_of(peer * qloc, qloc), qloc), :],
            dst_ref=arrived.at[me, pl.ds(2 * parent_at, 2)],
            send_sem=out_send.at[parent_at],
            recv_sem=out_recv.at[parent_at],
            device_id={"box": peer},
            device_id_type=MESH,
        )

    tile = 256
    def lift_parent(parent_at):
        def lift(t, carry):
            at = pl.multiple_of(t * tile, tile)
            left = interp_ref[:, pl.ds(at, tile)].T
            real = jnp.zeros((tile, illums), F32)
            imag = jnp.zeros((tile, illums), F32)
            for child in range(8):
                b = parent_at * 8 + child
                both = dot(left, jnp.concatenate([pat_ref[0, b], pat_ref[1, b]], axis=1))
                cosine = phase_ref[pl.ds(at, tile), child : child + 1]
                sine = phase_ref[pl.ds(at, tile), 8 + child : 9 + child]
                re, im = both[:, :illums], both[:, illums:]
                real = real + (cosine * re - sine * im)
                imag = imag + (cosine * im + sine * re)
            parent[2 * parent_at, pl.ds(at, tile), :] = real.astype(BF16)
            parent[2 * parent_at + 1, pl.ds(at, tile), :] = imag.astype(BF16)
            return carry

        lax.fori_loop(0, qdir // tile, lift, 0)

    def send_out(parent_at, low, high):
        def start_out(i, carry):
            out_copy(i, parent_at).start()
            return carry

        lax.fori_loop(low, high, start_out, 0)

    parents = n * groups8
    parents2 = 2 * parents

    def build_couple():
        lanes = lax.broadcasted_iota(jnp.int32, (parents, parents), 1)
        code = jnp.zeros((parents, parents), jnp.int32)
        slot_code = jnp.where(mask_ref[...] > 0, index_ref[...] + 1, 0).T
        slot_source = source_ref[...].T
        for j in range(source_ref.shape[0]):
            code = code + jnp.where(slot_source[:, j : j + 1] == lanes, slot_code[:, j : j + 1], 0)
        code = jnp.concatenate([code, code], axis=1) - 1
        each = max(1, 256 // parents2)
        kinds = lax.broadcasted_iota(jnp.int32, (par_ref.shape[1], each * parents2), 0)
        first = lax.broadcasted_iota(jnp.int32, (qloc, parents2), 1) < parents
        for p in range(0, parents, each):
            row = jnp.concatenate([code[p + u : p + u + 1] for u in range(each)], axis=1)
            hot = jnp.where(kinds == row, 1.0, 0.0).astype(BF16)
            got = [dot_rows(par_ref[part], hot) for part in range(2)]
            for u in range(each):
                real = got[0][:, u * parents2 : (u + 1) * parents2]
                imag = got[1][:, u * parents2 : (u + 1) * parents2]
                couple[pl.ds(p + u, qloc, stride=ppitch), :] = jnp.where(first, real, -imag)
                couple[pl.ds(parents + p + u, qloc, stride=ppitch), :] = jnp.where(first, imag, real)

    def build_op():
        sources = low_index_ref.shape[1]
        width = 2 * sources + -2 * sources % 128
        wanted = jnp.where(low_mask_ref[...] > 0, low_index_ref[...] + 1, 0)
        column = lax.broadcasted_iota(jnp.int32, (sources, width), 1)
        spread = lax.broadcasted_iota(jnp.int32, (sources, width), 0) == column // 16 * 8 + column % 8
        spread = jnp.where(spread, 1.0, 0.0).astype(BF16)
        high = dot((wanted // 16).astype(F32).astype(BF16), spread)
        rest = dot((wanted % 16).astype(F32).astype(BF16), spread)
        code = (16 * high + rest).astype(jnp.int32) - 1
        low_kinds = lax.broadcasted_iota(jnp.int32, (table_ref.shape[1], 2 * width), 0)
        low_first = lax.broadcasted_iota(jnp.int32, (kdir, width), 1) // 8 % 2 == 0
        for b in range(0, boxes, 2):
            row = jnp.concatenate([code[b : b + 1], code[b + 1 : b + 2]], axis=1)
            hot = jnp.where(low_kinds == row, 1.0, 0.0).astype(BF16)
            got = [dot_rows(table_ref[part], hot) for part in range(2)]
            for u in range(2):
                real = got[0][:, u * width : (u + 1) * width]
                imag = got[1][:, u * width : (u + 1) * width]
                op[pl.ds(b + u, kdir, stride=bpitch), :] = jnp.where(low_first, real, -imag)
                op[pl.ds(boxes + b + u, kdir, stride=bpitch), :] = jnp.where(low_first, imag, real)

    def widen(source, value):
        for part in range(2):
            for p in range(groups8):
                s = (part * n + source) * groups8 + p
                at = pl.multiple_of(s * qpitch, 8)
                wide[pl.ds(at, qloc), :] = value(p * 2 + part).astype(F32)

    def back_copy(i, parent_at):
        peer = lax.rem(me + i, n)
        return pltpu.make_async_remote_copy(
            src_ref=result_send.at[:, pl.ds(peer * groups8 + parent_at, 1)],
            dst_ref=returned.at[parent_at, :, :, pl.ds(pl.multiple_of(me * qloc, qloc), qloc), :],
            send_sem=back_send.at[parent_at],
            recv_sem=back_recv.at[parent_at],
            device_id={"box": peer},
            device_id_type=MESH,
        )

    def exchange():
        widen(me, lambda c: parent[c, pl.ds(pl.multiple_of(me * qloc, qloc), qloc), :])

        for parent_at in range(groups8):
            whole = arrived.at[pl.ds(0, n - 1), pl.ds(2 * parent_at, 2)]
            remote(whole, whole, out_send.at[parent_at], out_recv.at[parent_at], 0).wait()

        def take(i, carry):
            source = lax.rem(me - i + n, n)
            widen(source, lambda c: arrived[source, c])
            return carry

        lax.fori_loop(1, n, take, 0)

        def translate(t, carry):
            for u in range(unroll):
                q = t * unroll + u
                sources = wide[pl.ds(q, parents2, stride=qpitch), :].astype(BF16)
                result[pl.ds(q, parents2, stride=qpitch), :] = dot(
                    couple[pl.ds(pl.multiple_of(q * ppitch, 8), parents2), :].astype(BF16), sources
                )
            return carry

        lax.fori_loop(0, qloc // unroll, translate, 0)
        for s in range(parents2):
            result_send[s // parents, s % parents] = result[pl.ds(s * qpitch, qloc), :].astype(BF16)

    def send_back(parent_at, low, high):
        def start_back(i, carry):
            back_copy(i, parent_at).start()
            return carry

        lax.fori_loop(low, high, start_back, 0)

    def keep_back():
        mine = pl.ds(pl.multiple_of(me * qloc, qloc), qloc)
        for parent_at in range(groups8):
            returned[parent_at, :, :, mine, :] = result_send[:, pl.ds(me * groups8 + parent_at, 1)]

    def near(at):
        def one(t, carry):
            sums = []
            for u in range(unroll):
                k = at + t * unroll + u
                operator = op[pl.ds(pl.multiple_of(k * bpitch, 8), both_own), :].astype(BF16)
                sources = jnp.concatenate([own[k], far[k]], axis=0)
                sums.append(dot(operator[:, : both_own + 16 * listed], sources))
            for u in range(unroll):
                acc[pl.ds(at + t * unroll + u, both_own, stride=kpitch), :] = sums[u]
            return carry

        lax.fori_loop(0, span // unroll, one, 0)

    def down(parent_at):
        whole = returned.at[parent_at, :, :, pl.ds(0, (n - 1) * qloc), :]
        remote(whole, whole, back_send.at[parent_at], back_recv.at[parent_at], 0).wait()
        for child in range(8):
            b = parent_at * 8 + child
            re = returned[parent_at, 0, 0].astype(F32)
            im = returned[parent_at, 1, 0].astype(F32)
            cosine = phase_ref[:, child : child + 1]
            sine = phase_ref[:, 8 + child : 9 + child]
            real = (cosine * re + sine * im).astype(BF16)
            imag = (cosine * im - sine * re).astype(BF16)
            both = dot(interp_ref[...], jnp.concatenate([real, imag], axis=1))
            out_ref[pl.ds(b * kdir, kdir), :] = both[:, :illums]
            out_ref[pl.ds((boxes + b) * kdir, kdir), :] = both[:, illums:]

    def settle():
        for b in range(both_own):
            spots = pl.ds(b * kdir, kdir)
            out_ref[spots, :] = out_ref[spots, :] + acc[pl.ds(b * kpitch, kdir), :]

    last_step = 2 * deep + 1

    def far_step(chain, step):
        if step <= deep:
            reduce(chain, step)
        elif step < last_step:
            double(chain, last_step - step)
            if step == last_step - 1:
                near(core * (kdir // 2) + chain * span)
        else:
            doubling(chain, 0).wait()
            near((1 - core) * (kdir // 2) + chain * span)

    def far_slot(slot):
        for chain in reversed(range(chains)):
            if 0 <= slot - chain <= last_step:
                far_step(chain, slot - chain)

    slots = chains + last_step
    lift_parent(0)
    lift_parent(1)
    build_couple()
    build_op()
    pl.semaphore_wait(barrier, n - 1)
    for chain in range(chains): swap(chain).start()
    send_out(0, 1, n)
    for chain in range(chains): merge(chain)
    send_out(1, 1, n)
    far_slot(0)
    far_slot(1)
    far_slot(2)
    far_slot(3)
    far_slot(4)
    exchange()
    send_back(0, 1, n)
    send_back(1, 1, n)
    keep_back()
    far_slot(5)
    far_slot(6)
    down(0)
    far_slot(7)
    down(1)
    far_slot(8)
    settle()

def shards(
    patterns,
    owner_block,
    low_index,
    low_mask,
    low_table,
    interp,
    shift_angle,
    par_source,
    par_index,
    par_mask,
    par_table,
):
    boxes, kdir, illums = patterns.shape[1:]
    groups8 = boxes // 8
    qdir = interp.shape[1]
    n = lax.axis_size("box")
    listed = owner_block.shape[0]
    parents = par_source.shape[0]
    qloc = qdir // n
    sources = low_index.shape[1]
    chains = 4

    start = lax.axis_index("box") * qloc
    table = lax.dynamic_slice_in_dim(par_table, start, qloc, 2)

    pitches = (kdir + 8, 2 * boxes + 8, qloc + 8, 2 * parents + 8)
    kpitch, bpitch, qpitch, ppitch = pitches
    vmem = pl.BlockSpec(memory_space=pltpu.VMEM)
    smem = pl.BlockSpec(memory_space=pltpu.SMEM)
    stages = n.bit_length() - 1
    dma = pltpu.SemaphoreType.DMA
    return pl.pallas_call(
        functools.partial(kernel, n, listed, chains, pitches),
        out_shape=jax.ShapeDtypeStruct((2 * boxes * kdir, illums), F32),
        in_specs=[smem] + [vmem] * 10,
        out_specs=vmem,
        scratch_shapes=[
            pltpu.VMEM((qdir, 16), F32),
            pltpu.VMEM((kdir * bpitch, 2 * sources + -2 * sources % 128), F32),
            pltpu.VMEM((qloc * ppitch, 2 * parents), F32),
            pltpu.VMEM((2 * groups8, qdir, illums), BF16),
            pltpu.VMEM((n, 2 * groups8, qloc, illums), BF16),
            pltpu.VMEM((2 * parents * qpitch, illums), F32),
            pltpu.VMEM((2 * parents * qpitch, illums), F32),
            pltpu.VMEM((2, parents, qloc, illums), BF16),
            pltpu.VMEM((groups8, 2, 1, qdir, illums), BF16),
            pltpu.VMEM((kdir, 2 * boxes, illums), BF16),
            [pltpu.VMEM((kdir // 2 // chains, 2 * boxes, illums), BF16) for _ in range(chains)],
            pltpu.VMEM((kdir, 16 * listed, illums), BF16),
            pltpu.VMEM((kdir // 2, 16 * listed, illums), BF16),
            pltpu.VMEM((kdir, 16 * listed, illums), BF16),
            pltpu.VMEM((2 * boxes * kpitch, illums), F32),
            pltpu.VMEM((2 * boxes * kpitch, illums), F32),
            dma((groups8,)),
            dma((groups8,)),
            dma((groups8,)),
            dma((groups8,)),
            dma((chains,)),
            dma((chains,)),
            dma((chains, stages - 1)),
            dma((chains, stages - 1)),
            dma((chains, stages - 1)),
            dma((chains, stages - 1)),
        ],
        compiler_params=pltpu.CompilerParams(
            collective_id=0, has_side_effects=True, vmem_limit_bytes=56 * 1024 * 1024
        ),
    )(
        owner_block,
        patterns,
        low_index,
        low_mask,
        low_table,
        par_source.T,
        par_index.T,
        par_mask.T,
        table,
        interp,
        shift_angle,
    ).reshape(2, boxes, kdir, illums)


def solution(mesh):
    placed = (
        P(None, "box", None, "illum"),
        P(),
        P("box", None),
        P("box", None),
        P(),
        P(),
        P(),
        P(),
        P(),
        P(),
        P(),
    )
    return jax.shard_map(
        shards, mesh=mesh, in_specs=placed, out_specs=P(None, "box", None, "illum"), check_vma=False
    )
```

```python
import functools

import jax
import jax.numpy as jnp
from jax import lax
from jax.experimental import pallas as pl
from jax.experimental.pallas import tpu as pltpu
from jax.sharding import PartitionSpec as P

F32 = jnp.float32
BF16 = jnp.bfloat16
MESH = pl.DeviceIdType.MESH


def dot(left, right):
    return jnp.dot(left, right, preferred_element_type=F32)


def dot_rows(left, right):
    return lax.dot_general(left, right, (((0,), (0,)), ((), ())), preferred_element_type=F32)


def kernel(
    n,
    listed,
    chains,
    pitches,
    owner_ref,
    pat_ref,
    low_index_ref,
    low_mask_ref,
    table_ref,
    source_ref,
    index_ref,
    mask_ref,
    par_ref,
    interp_ref,
    angle_ref,
    out_ref,
    phase_ref,
    op,
    couple,
    parent,
    arrived,
    wide,
    result,
    result_send,
    returned,
    own,
    given,
    buf,
    landed,
    far,
    own_wide,
    acc,
    out_send,
    out_recv,
    back_send,
    back_recv,
    swap_send,
    swap_recv,
    rs_send,
    rs_recv,
    ag_send,
    ag_recv,
):
    me = lax.axis_index("box")
    core = me % 2
    boxes = pat_ref.shape[1]
    kdir, illums = pat_ref.shape[2], pat_ref.shape[3]
    groups8 = boxes // 8
    qdir = interp_ref.shape[1]
    qloc = qdir // n
    both_own = 2 * boxes
    span = kdir // 2 // chains
    bits = list(range(1, n.bit_length() - 1))
    orders = [bits for _ in range(chains)]
    deep = len(bits) - 1
    kpitch, bpitch, qpitch, ppitch = pitches

    barrier = pltpu.get_barrier_semaphore()

    def greet(i, carry):
        peer = lax.rem(me + i, n)
        pl.semaphore_signal(barrier, inc=1, device_id={"box": peer}, device_id_type=MESH)
        return carry

    lax.fori_loop(1, n, greet, 0)

    unroll = 8
    for part in range(2):
        for b in range(boxes):
            spot = b // 8 * 16 + part * 8 + b % 8
            own_wide[pl.ds(spot * kpitch, kdir), :] = pat_ref[part, b].astype(F32)

    def turn(t, carry):
        for u in range(unroll):
            k = t * unroll + u
            own[k] = own_wide[pl.ds(k, both_own, stride=kpitch), :].astype(BF16)
        return carry

    lax.fori_loop(0, kdir // unroll, turn, 0)

    def remote(src, dst, send, recv, bit):
        mine = me // (1 << bit) % 2
        return pltpu.make_async_remote_copy(
            src_ref=src,
            dst_ref=dst,
            send_sem=send,
            recv_sem=recv,
            device_id={"box": me + (1 - 2 * mine) * (1 << bit)},
            device_id_type=MESH,
        )

    def swap(chain):
        spots = own.at[pl.ds((1 - core) * (kdir // 2) + chain * span, span)]
        return remote(spots, given[chain], swap_send.at[chain], swap_recv.at[chain], 0)

    def place(chain, depth):
        low = core * (kdir // 2) + chain * span
        size = span
        for b in orders[chain][:depth]:
            size = size // 2
            low = low + me // (1 << b) % 2 * size
        return low, size

    def reduction(chain, depth):
        bit = orders[chain][depth]
        low, size = place(chain, depth)
        if depth < deep:
            size = size // 2
            low = low + (1 - me // (1 << bit) % 2) * size
        spot = chain * span + span - (span >> depth)
        return remote(
            buf.at[pl.ds(low, size)],
            landed.at[pl.ds(spot, size)],
            rs_send.at[chain, depth],
            rs_recv.at[chain, depth],
            bit,
        )

    def reduce(chain, depth):
        reduction(chain, depth).wait()
        low, size = place(chain, min(depth + 1, deep))
        spot = chain * span + span - (span >> depth)
        target = far if depth == deep else buf
        target[pl.ds(low, size)] = buf[pl.ds(low, size)] + landed[pl.ds(spot, size)]
        if depth < deep:
            reduction(chain, depth + 1).start()
        else:
            doubling(chain, deep).start()

    def doubling(chain, depth):
        low, size = place(chain, depth)
        bit = orders[chain][depth - 1] if depth else 0
        spots = far.at[pl.ds(low, size)]
        return remote(spots, spots, ag_send.at[chain, depth], ag_recv.at[chain, depth], bit)

    def double(chain, depth):
        doubling(chain, depth).wait()
        doubling(chain, depth - 1).start()

    def merge(chain):
        swap(chain).wait()
        low, size = place(chain, 0)
        for step in range(listed):
            owner = owner_ref[step]
            device = owner // groups8
            rows = pl.ds(owner % groups8 * 16, 16)
            block = own[pl.ds(low, size), rows, :]
            theirs = given[chain][:, rows, :]
            block = jnp.where(device == me, block, jnp.where(device // 2 == me // 2, theirs, jnp.zeros_like(block)))
            buf[pl.ds(low, size), step * 16 : step * 16 + 16, :] = block
        reduction(chain, 0).start()

    phase_ref[:, :8] = jnp.cos(angle_ref[...]).T
    phase_ref[:, 8:] = jnp.sin(angle_ref[...]).T

    def peer_of(i):
        peer = me
        for b in range(n.bit_length() - 1):
            if i >> b & 1:
                peer = peer + (1 - 2 * (me // (1 << b) % 2)) * (1 << b)
        return peer

    tour = list(range(n - 1, 0, -1))

    def out_copy(i, parent_at):
        peer = peer_of(i)
        return pltpu.make_async_remote_copy(
            src_ref=parent.at[pl.ds(2 * parent_at, 2), pl.ds(pl.multiple_of(peer * qloc, qloc), qloc), :],
            dst_ref=arrived.at[me, pl.ds(2 * parent_at, 2)],
            send_sem=out_send.at[parent_at],
            recv_sem=out_recv.at[parent_at],
            device_id={"box": peer},
            device_id_type=MESH,
        )

    tile = 256
    def lift_parent(parent_at):
        def lift(t, carry):
            at = pl.multiple_of(t * tile, tile)
            left = interp_ref[:, pl.ds(at, tile)].T
            real = jnp.zeros((tile, illums), F32)
            imag = jnp.zeros((tile, illums), F32)
            for child in range(8):
                b = parent_at * 8 + child
                both = dot(left, jnp.concatenate([pat_ref[0, b], pat_ref[1, b]], axis=1))
                cosine = phase_ref[pl.ds(at, tile), child : child + 1]
                sine = phase_ref[pl.ds(at, tile), 8 + child : 9 + child]
                re, im = both[:, :illums], both[:, illums:]
                real = real + (cosine * re - sine * im)
                imag = imag + (cosine * im + sine * re)
            parent[2 * parent_at, pl.ds(at, tile), :] = real.astype(BF16)
            parent[2 * parent_at + 1, pl.ds(at, tile), :] = imag.astype(BF16)
            return carry

        lax.fori_loop(0, qdir // tile, lift, 0)

    def send_out(parent_at):
        for i in tour:
            out_copy(i, parent_at).start()

    parents = n * groups8
    parents2 = 2 * parents

    def build_couple():
        lanes = lax.broadcasted_iota(jnp.int32, (parents, parents), 1)
        code = jnp.zeros((parents, parents), jnp.int32)
        slot_code = jnp.where(mask_ref[...] > 0, index_ref[...] + 1, 0).T
        slot_source = source_ref[...].T
        for j in range(source_ref.shape[0]):
            code = code + jnp.where(slot_source[:, j : j + 1] == lanes, slot_code[:, j : j + 1], 0)
        code = jnp.concatenate([code, code], axis=1) - 1
        each = max(1, 256 // parents2)
        kinds = lax.broadcasted_iota(jnp.int32, (par_ref.shape[1], each * parents2), 0)
        first = lax.broadcasted_iota(jnp.int32, (qloc, parents2), 1) < parents
        for p in range(0, parents, each):
            row = jnp.concatenate([code[p + u : p + u + 1] for u in range(each)], axis=1)
            hot = jnp.where(kinds == row, 1.0, 0.0).astype(BF16)
            got = [dot_rows(par_ref[part], hot) for part in range(2)]
            for u in range(each):
                real = got[0][:, u * parents2 : (u + 1) * parents2]
                imag = got[1][:, u * parents2 : (u + 1) * parents2]
                couple[pl.ds(p + u, qloc, stride=ppitch), :] = jnp.where(first, real, -imag)
                couple[pl.ds(parents + p + u, qloc, stride=ppitch), :] = jnp.where(first, imag, real)

    def build_op():
        sources = low_index_ref.shape[1]
        width = 2 * sources + -2 * sources % 128
        wanted = jnp.where(low_mask_ref[...] > 0, low_index_ref[...] + 1, 0)
        column = lax.broadcasted_iota(jnp.int32, (sources, width), 1)
        spread = lax.broadcasted_iota(jnp.int32, (sources, width), 0) == column // 16 * 8 + column % 8
        spread = jnp.where(spread, 1.0, 0.0).astype(BF16)
        high = dot((wanted // 16).astype(F32).astype(BF16), spread)
        rest = dot((wanted % 16).astype(F32).astype(BF16), spread)
        code = (16 * high + rest).astype(jnp.int32) - 1
        low_kinds = lax.broadcasted_iota(jnp.int32, (table_ref.shape[1], 2 * width), 0)
        low_first = lax.broadcasted_iota(jnp.int32, (kdir, width), 1) // 8 % 2 == 0
        for b in range(0, boxes, 2):
            row = jnp.concatenate([code[b : b + 1], code[b + 1 : b + 2]], axis=1)
            hot = jnp.where(low_kinds == row, 1.0, 0.0).astype(BF16)
            got = [dot_rows(table_ref[part], hot) for part in range(2)]
            for u in range(2):
                real = got[0][:, u * width : (u + 1) * width]
                imag = got[1][:, u * width : (u + 1) * width]
                op[pl.ds(b + u, kdir, stride=bpitch), :] = jnp.where(low_first, real, -imag)
                op[pl.ds(boxes + b + u, kdir, stride=bpitch), :] = jnp.where(low_first, imag, real)

    def widen(source, value):
        for part in range(2):
            for p in range(groups8):
                s = (part * n + source) * groups8 + p
                at = pl.multiple_of(s * qpitch, 8)
                wide[pl.ds(at, qloc), :] = value(p * 2 + part).astype(F32)

    def back_copy(i, parent_at):
        peer = peer_of(i)
        return pltpu.make_async_remote_copy(
            src_ref=result_send.at[:, pl.ds(peer * groups8 + parent_at, 1)],
            dst_ref=returned.at[parent_at, :, :, pl.ds(pl.multiple_of(me * qloc, qloc), qloc), :],
            send_sem=back_send.at[parent_at],
            recv_sem=back_recv.at[parent_at],
            device_id={"box": peer},
            device_id_type=MESH,
        )

    def exchange():
        widen(me, lambda c: parent[c, pl.ds(pl.multiple_of(me * qloc, qloc), qloc), :])

        for parent_at in range(groups8):
            whole = arrived.at[pl.ds(0, n - 1), pl.ds(2 * parent_at, 2)]
            remote(whole, whole, out_send.at[parent_at], out_recv.at[parent_at], 0).wait()

        def take(i, carry):
            source = lax.rem(me - i + n, n)
            widen(source, lambda c: arrived[source, c])
            return carry

        lax.fori_loop(1, n, take, 0)

        def translate(t, carry):
            for u in range(unroll):
                q = t * unroll + u
                sources = wide[pl.ds(q, parents2, stride=qpitch), :].astype(BF16)
                result[pl.ds(q, parents2, stride=qpitch), :] = dot(
                    couple[pl.ds(pl.multiple_of(q * ppitch, 8), parents2), :].astype(BF16), sources
                )
            return carry

        lax.fori_loop(0, qloc // unroll, translate, 0)
        for s in range(parents2):
            result_send[s // parents, s % parents] = result[pl.ds(s * qpitch, qloc), :].astype(BF16)

    def send_back(parent_at):
        for i in tour:
            back_copy(i, parent_at).start()

    def keep_back():
        mine = pl.ds(pl.multiple_of(me * qloc, qloc), qloc)
        for parent_at in range(groups8):
            returned[parent_at, :, :, mine, :] = result_send[:, pl.ds(me * groups8 + parent_at, 1)]

    def near(at):
        def one(t, carry):
            sums = []
            for u in range(unroll):
                k = at + t * unroll + u
                operator = op[pl.ds(pl.multiple_of(k * bpitch, 8), both_own), :].astype(BF16)
                sources = jnp.concatenate([own[k], far[k]], axis=0)
                sums.append(dot(operator[:, : both_own + 16 * listed], sources))
            for u in range(unroll):
                acc[pl.ds(at + t * unroll + u, both_own, stride=kpitch), :] = sums[u]
            return carry

        lax.fori_loop(0, span // unroll, one, 0)

    def down(parent_at):
        whole = returned.at[parent_at, :, :, pl.ds(0, (n - 1) * qloc), :]
        remote(whole, whole, back_send.at[parent_at], back_recv.at[parent_at], 0).wait()
        for child in range(8):
            b = parent_at * 8 + child
            re = returned[parent_at, 0, 0].astype(F32)
            im = returned[parent_at, 1, 0].astype(F32)
            cosine = phase_ref[:, child : child + 1]
            sine = phase_ref[:, 8 + child : 9 + child]
            real = (cosine * re + sine * im).astype(BF16)
            imag = (cosine * im - sine * re).astype(BF16)
            both = dot(interp_ref[...], jnp.concatenate([real, imag], axis=1))
            out_ref[pl.ds(b * kdir, kdir), :] = both[:, :illums]
            out_ref[pl.ds((boxes + b) * kdir, kdir), :] = both[:, illums:]

    def settle():
        for b in range(both_own):
            spots = pl.ds(b * kdir, kdir)
            out_ref[spots, :] = out_ref[spots, :] + acc[pl.ds(b * kpitch, kdir), :]

    last_step = 2 * deep + 1

    def far_step(chain, step):
        if step <= deep:
            reduce(chain, step)
        elif step < last_step:
            double(chain, last_step - step)
        else:
            doubling(chain, 0).wait()

    def far_slot(slot):
        live = [chain for chain in reversed(range(chains)) if 0 <= slot - chain <= last_step]
        for chain in live:
            far_step(chain, slot - chain)
        for chain in live:
            if slot - chain == last_step - 1:
                near(core * (kdir // 2) + chain * span)
            if slot - chain == last_step:
                near((1 - core) * (kdir // 2) + chain * span)

    slots = chains + last_step
    for parent_at in range(groups8):
        lift_parent(parent_at)
    build_couple()
    build_op()
    pl.semaphore_wait(barrier, n - 1)
    for chain in range(chains):
        swap(chain).start()
    send_out(0)
    for chain in range(chains):
        merge(chain)
    for parent_at in range(1, groups8):
        send_out(parent_at)
    for slot in range(slots - 4):
        far_slot(slot)
    exchange()
    for parent_at in range(groups8):
        send_back(parent_at)
    keep_back()
    far_slot(slots - 4)
    far_slot(slots - 3)
    down(0)
    far_slot(slots - 2)
    for parent_at in range(1, groups8):
        down(parent_at)
    far_slot(slots - 1)
    settle()


def shards(
    patterns,
    owner_block,
    low_index,
    low_mask,
    low_table,
    interp,
    shift_angle,
    par_source,
    par_index,
    par_mask,
    par_table,
):
    boxes, kdir, illums = patterns.shape[1:]
    groups8 = boxes // 8
    qdir = interp.shape[1]
    n = lax.axis_size("box")
    listed = owner_block.shape[0]
    parents = par_source.shape[0]
    qloc = qdir // n
    sources = low_index.shape[1]
    chains = 4

    start = lax.axis_index("box") * qloc
    table = lax.dynamic_slice_in_dim(par_table, start, qloc, 2)

    pitches = (kdir + 8, 2 * boxes + 8, qloc + 8, 2 * parents + 8)
    kpitch, bpitch, qpitch, ppitch = pitches
    vmem = pl.BlockSpec(memory_space=pltpu.VMEM)
    smem = pl.BlockSpec(memory_space=pltpu.SMEM)
    stages = n.bit_length() - 1
    dma = pltpu.SemaphoreType.DMA
    return pl.pallas_call(
        functools.partial(kernel, n, listed, chains, pitches),
        out_shape=jax.ShapeDtypeStruct((2 * boxes * kdir, illums), F32),
        in_specs=[smem] + [vmem] * 10,
        out_specs=vmem,
        scratch_shapes=[
            pltpu.VMEM((qdir, 16), F32),
            pltpu.VMEM((kdir * bpitch, 2 * sources + -2 * sources % 128), F32),
            pltpu.VMEM((qloc * ppitch, 2 * parents), F32),
            pltpu.VMEM((2 * groups8, qdir, illums), BF16),
            pltpu.VMEM((n, 2 * groups8, qloc, illums), BF16),
            pltpu.VMEM((2 * parents * qpitch, illums), F32),
            pltpu.VMEM((2 * parents * qpitch, illums), F32),
            pltpu.VMEM((2, parents, qloc, illums), BF16),
            pltpu.VMEM((groups8, 2, 1, qdir, illums), BF16),
            pltpu.VMEM((kdir, 2 * boxes, illums), BF16),
            [pltpu.VMEM((kdir // 2 // chains, 2 * boxes, illums), BF16) for _ in range(chains)],
            pltpu.VMEM((kdir, 16 * listed, illums), BF16),
            pltpu.VMEM((kdir // 2, 16 * listed, illums), BF16),
            pltpu.VMEM((kdir, 16 * listed, illums), BF16),
            pltpu.VMEM((2 * boxes * kpitch, illums), F32),
            pltpu.VMEM((2 * boxes * kpitch, illums), F32),
            dma((groups8,)),
            dma((groups8,)),
            dma((groups8,)),
            dma((groups8,)),
            dma((chains,)),
            dma((chains,)),
            dma((chains, stages - 1)),
            dma((chains, stages - 1)),
            dma((chains, stages - 1)),
            dma((chains, stages - 1)),
        ],
        compiler_params=pltpu.CompilerParams(
            collective_id=0, has_side_effects=True, vmem_limit_bytes=56 * 1024 * 1024
        ),
    )(
        owner_block,
        patterns,
        low_index,
        low_mask,
        low_table,
        par_source.T,
        par_index.T,
        par_mask.T,
        table,
        interp,
        shift_angle,
    ).reshape(2, boxes, kdir, illums)


def solution(mesh):
    placed = (
        P(None, "box", None, "illum"),
        P(),
        P("box", None),
        P("box", None),
        P(),
        P(),
        P(),
        P(),
        P(),
        P(),
        P(),
    )
    return jax.shard_map(
        shards, mesh=mesh, in_specs=placed, out_specs=P(None, "box", None, "illum"), check_vma=False
    )
```

```python
import functools

import jax
import jax.numpy as jnp
from jax import lax
from jax.experimental import pallas as pl
from jax.experimental.pallas import tpu as pltpu
from jax.sharding import PartitionSpec as P

F32 = jnp.float32
BF16 = jnp.bfloat16
MESH = pl.DeviceIdType.MESH


def dot(left, right):
    return jnp.dot(left, right, preferred_element_type=F32)


def dot_rows(left, right):
    return lax.dot_general(left, right, (((0,), (0,)), ((), ())), preferred_element_type=F32)


def kernel(
    n,
    listed,
    chains,
    pitches,
    owner_ref,
    pat_ref,
    low_index_ref,
    low_mask_ref,
    table_ref,
    source_ref,
    index_ref,
    mask_ref,
    par_ref,
    interp_ref,
    angle_ref,
    out_ref,
    low_wide,
    par_wide,
    phase_ref,
    op,
    couple,
    parent,
    arrived,
    wide,
    result,
    result_send,
    returned,
    own,
    given,
    buf,
    landed,
    far,
    own_wide,
    acc,
    out_send,
    out_recv,
    back_send,
    back_recv,
    swap_send,
    swap_recv,
    rs_send,
    rs_recv,
    ag_send,
    ag_recv,
):
    me = lax.axis_index("box")
    core = me % 2
    boxes = pat_ref.shape[1]
    kdir, illums = pat_ref.shape[2], pat_ref.shape[3]
    groups8 = boxes // 8
    qdir = interp_ref.shape[1]
    qloc = qdir // n
    both_own = 2 * boxes
    span = kdir // 2 // chains
    bits = list(range(1, n.bit_length() - 1))
    orders = [bits for _ in range(chains)]
    deep = len(bits) - 1
    kpitch, bpitch, qpitch, ppitch = pitches

    barrier = pltpu.get_barrier_semaphore()

    def greet(i, carry):
        peer = lax.rem(me + i, n)
        pl.semaphore_signal(barrier, inc=1, device_id={"box": peer}, device_id_type=MESH)
        return carry

    lax.fori_loop(1, n, greet, 0)

    unroll = 8
    for part in range(2):
        for b in range(boxes):
            spot = b // 8 * 16 + part * 8 + b % 8
            own_wide[pl.ds(spot * kpitch, kdir), :] = pat_ref[part, b].astype(F32)

    def turn(t, carry):
        for u in range(unroll):
            k = t * unroll + u
            own[k] = own_wide[pl.ds(k, both_own, stride=kpitch), :].astype(BF16)
        return carry

    lax.fori_loop(0, kdir // unroll, turn, 0)

    def remote(src, dst, send, recv, bit):
        mine = me // (1 << bit) % 2
        return pltpu.make_async_remote_copy(
            src_ref=src,
            dst_ref=dst,
            send_sem=send,
            recv_sem=recv,
            device_id={"box": me + (1 - 2 * mine) * (1 << bit)},
            device_id_type=MESH,
        )

    def swap(chain):
        spots = own.at[pl.ds((1 - core) * (kdir // 2) + chain * span, span)]
        return remote(spots, given[chain], swap_send.at[chain], swap_recv.at[chain], 0)

    def place(chain, depth):
        low = core * (kdir // 2) + chain * span
        size = span
        for b in orders[chain][:depth]:
            size = size // 2
            low = low + me // (1 << b) % 2 * size
        return low, size

    def reduction(chain, depth):
        bit = orders[chain][depth]
        low, size = place(chain, depth)
        if depth < deep:
            size = size // 2
            low = low + (1 - me // (1 << bit) % 2) * size
        spot = chain * span + span - (span >> depth)
        return remote(
            buf.at[pl.ds(low, size)],
            landed.at[pl.ds(spot, size)],
            rs_send.at[chain, depth],
            rs_recv.at[chain, depth],
            bit,
        )

    def reduce(chain, depth):
        reduction(chain, depth).wait()
        low, size = place(chain, min(depth + 1, deep))
        spot = chain * span + span - (span >> depth)
        target = far if depth == deep else buf
        target[pl.ds(low, size)] = buf[pl.ds(low, size)] + landed[pl.ds(spot, size)]
        if depth < deep:
            reduction(chain, depth + 1).start()
        else:
            doubling(chain, deep).start()

    def doubling(chain, depth):
        low, size = place(chain, depth)
        bit = orders[chain][depth - 1] if depth else 0
        spots = far.at[pl.ds(low, size)]
        return remote(spots, spots, ag_send.at[chain, depth], ag_recv.at[chain, depth], bit)

    def double(chain, depth):
        doubling(chain, depth).wait()
        doubling(chain, depth - 1).start()

    def merge(chain):
        swap(chain).wait()
        low, size = place(chain, 0)
        for step in range(listed):
            owner = owner_ref[step]
            device = owner // groups8
            rows = pl.ds(owner % groups8 * 16, 16)
            block = own[pl.ds(low, size), rows, :]
            theirs = given[chain][:, rows, :]
            block = jnp.where(device == me, block, jnp.where(device // 2 == me // 2, theirs, jnp.zeros_like(block)))
            buf[pl.ds(low, size), step * 16 : step * 16 + 16, :] = block
        reduction(chain, 0).start()

    phase_ref[:, :8] = jnp.cos(angle_ref[...]).T
    phase_ref[:, 8:] = jnp.sin(angle_ref[...]).T

    def peer_of(i):
        peer = me
        for b in range(n.bit_length() - 1):
            if i >> b & 1:
                peer = peer + (1 - 2 * (me // (1 << b) % 2)) * (1 << b)
        return peer

    tour = list(range(n - 1, 0, -1))

    def out_copy(i, parent_at):
        peer = peer_of(i)
        return pltpu.make_async_remote_copy(
            src_ref=parent.at[pl.ds(2 * parent_at, 2), pl.ds(pl.multiple_of(peer * qloc, qloc), qloc), :],
            dst_ref=arrived.at[me, pl.ds(2 * parent_at, 2)],
            send_sem=out_send.at[parent_at],
            recv_sem=out_recv.at[parent_at],
            device_id={"box": peer},
            device_id_type=MESH,
        )

    tile = 256
    def lift_parent(parent_at):
        def lift(t, carry):
            at = pl.multiple_of(t * tile, tile)
            left = interp_ref[:, pl.ds(at, tile)].T
            real = jnp.zeros((tile, illums), F32)
            imag = jnp.zeros((tile, illums), F32)
            for child in range(8):
                b = parent_at * 8 + child
                both = dot(left, jnp.concatenate([pat_ref[0, b], pat_ref[1, b]], axis=1))
                cosine = phase_ref[pl.ds(at, tile), child : child + 1]
                sine = phase_ref[pl.ds(at, tile), 8 + child : 9 + child]
                re, im = both[:, :illums], both[:, illums:]
                real = real + (cosine * re - sine * im)
                imag = imag + (cosine * im + sine * re)
            parent[2 * parent_at, pl.ds(at, tile), :] = real.astype(BF16)
            parent[2 * parent_at + 1, pl.ds(at, tile), :] = imag.astype(BF16)
            return carry

        lax.fori_loop(0, qdir // tile, lift, 0)

    def send_out(parent_at):
        for i in tour:
            out_copy(i, parent_at).start()

    parents = n * groups8
    parents2 = 2 * parents

    def build_couple():
        lanes = lax.broadcasted_iota(jnp.int32, (parents, parents), 1)
        code = jnp.zeros((parents, parents), jnp.int32)
        slot_code = jnp.where(mask_ref[...] > 0, index_ref[...] + 1, 0).T
        slot_source = source_ref[...].T
        for j in range(source_ref.shape[0]):
            code = code + jnp.where(slot_source[:, j : j + 1] == lanes, slot_code[:, j : j + 1], 0)
        code = jnp.concatenate([code, code], axis=1) - 1
        each = max(1, 256 // parents2)
        par_wide[...] = par_ref[...].astype(F32)
        lines = qdir // 128 * 2
        entries = par_ref.shape[0] // lines
        start = me * qloc
        tables = []
        for part in range(2):
            wanted = par_wide[pl.ds(start // 128 * 2 + part, entries, stride=lines), :]
            tables.append(pltpu.roll(wanted, (128 - start % 128) % 128, 1)[:, :qloc].astype(BF16))
        kinds = lax.broadcasted_iota(jnp.int32, (entries, each * parents2), 0)
        first = lax.broadcasted_iota(jnp.int32, (qloc, parents2), 1) < parents
        for p in range(0, parents, each):
            row = jnp.concatenate([code[p + u : p + u + 1] for u in range(each)], axis=1)
            hot = jnp.where(kinds == row, 1.0, 0.0).astype(BF16)
            got = [dot_rows(tables[part], hot) for part in range(2)]
            for u in range(each):
                real = got[0][:, u * parents2 : (u + 1) * parents2]
                imag = got[1][:, u * parents2 : (u + 1) * parents2]
                couple[pl.ds(p + u, qloc, stride=ppitch), :] = jnp.where(first, real, -imag)
                couple[pl.ds(parents + p + u, qloc, stride=ppitch), :] = jnp.where(first, imag, real)

    def build_op():
        sources = low_index_ref.shape[1]
        width = 2 * sources + -2 * sources % 128
        wanted = jnp.where(low_mask_ref[...] > 0, low_index_ref[...] + 1, 0)
        column = lax.broadcasted_iota(jnp.int32, (sources, width), 1)
        spread = lax.broadcasted_iota(jnp.int32, (sources, width), 0) == column // 16 * 8 + column % 8
        spread = jnp.where(spread, 1.0, 0.0).astype(BF16)
        high = dot((wanted // 16).astype(F32).astype(BF16), spread)
        rest = dot((wanted % 16).astype(F32).astype(BF16), spread)
        code = (16 * high + rest).astype(jnp.int32) - 1
        low_wide[...] = table_ref[...].astype(F32)
        entries = table_ref.shape[0] // 2
        tables = [low_wide[pl.ds(part, entries, stride=2), :].astype(BF16) for part in range(2)]
        low_kinds = lax.broadcasted_iota(jnp.int32, (entries, 2 * width), 0)
        low_first = lax.broadcasted_iota(jnp.int32, (kdir, width), 1) // 8 % 2 == 0
        for b in range(0, boxes, 2):
            row = jnp.concatenate([code[b : b + 1], code[b + 1 : b + 2]], axis=1)
            hot = jnp.where(low_kinds == row, 1.0, 0.0).astype(BF16)
            got = [dot_rows(tables[part], hot) for part in range(2)]
            for u in range(2):
                real = got[0][:, u * width : (u + 1) * width]
                imag = got[1][:, u * width : (u + 1) * width]
                op[pl.ds(b + u, kdir, stride=bpitch), :] = jnp.where(low_first, real, -imag)
                op[pl.ds(boxes + b + u, kdir, stride=bpitch), :] = jnp.where(low_first, imag, real)

    def widen(source, value):
        for part in range(2):
            for p in range(groups8):
                s = (part * n + source) * groups8 + p
                at = pl.multiple_of(s * qpitch, 8)
                wide[pl.ds(at, qloc), :] = value(p * 2 + part).astype(F32)

    def back_copy(i, parent_at):
        peer = peer_of(i)
        return pltpu.make_async_remote_copy(
            src_ref=result_send.at[:, pl.ds(peer * groups8 + parent_at, 1)],
            dst_ref=returned.at[parent_at, :, :, pl.ds(pl.multiple_of(me * qloc, qloc), qloc), :],
            send_sem=back_send.at[parent_at],
            recv_sem=back_recv.at[parent_at],
            device_id={"box": peer},
            device_id_type=MESH,
        )

    def exchange():
        widen(me, lambda c: parent[c, pl.ds(pl.multiple_of(me * qloc, qloc), qloc), :])

        for parent_at in range(groups8):
            whole = arrived.at[pl.ds(0, n - 1), pl.ds(2 * parent_at, 2)]
            remote(whole, whole, out_send.at[parent_at], out_recv.at[parent_at], 0).wait()

        def take(i, carry):
            source = lax.rem(me - i + n, n)
            widen(source, lambda c: arrived[source, c])
            return carry

        lax.fori_loop(1, n, take, 0)

        def translate(t, carry):
            for u in range(unroll):
                q = t * unroll + u
                sources = wide[pl.ds(q, parents2, stride=qpitch), :].astype(BF16)
                result[pl.ds(q, parents2, stride=qpitch), :] = dot(
                    couple[pl.ds(pl.multiple_of(q * ppitch, 8), parents2), :].astype(BF16), sources
                )
            return carry

        lax.fori_loop(0, qloc // unroll, translate, 0)
        for s in range(parents2):
            result_send[s // parents, s % parents] = result[pl.ds(s * qpitch, qloc), :].astype(BF16)

    def send_back(parent_at):
        for i in tour:
            back_copy(i, parent_at).start()

    def keep_back():
        mine = pl.ds(pl.multiple_of(me * qloc, qloc), qloc)
        for parent_at in range(groups8):
            returned[parent_at, :, :, mine, :] = result_send[:, pl.ds(me * groups8 + parent_at, 1)]

    def near(at):
        def one(t, carry):
            sums = []
            for u in range(unroll):
                k = at + t * unroll + u
                operator = op[pl.ds(pl.multiple_of(k * bpitch, 8), both_own), :].astype(BF16)
                sources = jnp.concatenate([own[k], far[k]], axis=0)
                sums.append(dot(operator[:, : both_own + 16 * listed], sources))
            for u in range(unroll):
                acc[pl.ds(at + t * unroll + u, both_own, stride=kpitch), :] = sums[u]
            return carry

        lax.fori_loop(0, span // unroll, one, 0)

    def down(parent_at):
        whole = returned.at[parent_at, :, :, pl.ds(0, (n - 1) * qloc), :]
        remote(whole, whole, back_send.at[parent_at], back_recv.at[parent_at], 0).wait()
        for child in range(8):
            b = parent_at * 8 + child
            re = returned[parent_at, 0, 0].astype(F32)
            im = returned[parent_at, 1, 0].astype(F32)
            cosine = phase_ref[:, child : child + 1]
            sine = phase_ref[:, 8 + child : 9 + child]
            real = (cosine * re + sine * im).astype(BF16)
            imag = (cosine * im - sine * re).astype(BF16)
            both = dot(interp_ref[...], jnp.concatenate([real, imag], axis=1))
            out_ref[pl.ds(b * kdir, kdir), :] = both[:, :illums]
            out_ref[pl.ds((boxes + b) * kdir, kdir), :] = both[:, illums:]

    def settle():
        for b in range(both_own):
            spots = pl.ds(b * kdir, kdir)
            out_ref[spots, :] = out_ref[spots, :] + acc[pl.ds(b * kpitch, kdir), :]

    last_step = 2 * deep + 1

    def far_step(chain, step):
        if step <= deep:
            reduce(chain, step)
        elif step < last_step:
            double(chain, last_step - step)
        else:
            doubling(chain, 0).wait()

    def far_slot(slot):
        live = [chain for chain in reversed(range(chains)) if 0 <= slot - chain <= last_step]
        for chain in live:
            far_step(chain, slot - chain)
        for chain in live:
            if slot - chain == last_step - 1:
                near(core * (kdir // 2) + chain * span)
            if slot - chain == last_step:
                near((1 - core) * (kdir // 2) + chain * span)

    slots = chains + last_step
    for parent_at in range(groups8):
        lift_parent(parent_at)
    build_couple()
    build_op()
    pl.semaphore_wait(barrier, n - 1)
    for chain in range(chains):
        swap(chain).start()
    send_out(0)
    for chain in range(chains):
        merge(chain)
    for parent_at in range(1, groups8):
        send_out(parent_at)
    for slot in range(slots - 4):
        far_slot(slot)
    exchange()
    for parent_at in range(groups8):
        send_back(parent_at)
    keep_back()
    far_slot(slots - 4)
    far_slot(slots - 3)
    down(0)
    far_slot(slots - 2)
    for parent_at in range(1, groups8):
        down(parent_at)
    far_slot(slots - 1)
    settle()


def shards(
    patterns,
    owner_block,
    low_index,
    low_mask,
    low_table,
    interp,
    shift_angle,
    par_source,
    par_index,
    par_mask,
    par_table,
):
    boxes, kdir, illums = patterns.shape[1:]
    groups8 = boxes // 8
    qdir = interp.shape[1]
    n = lax.axis_size("box")
    listed = owner_block.shape[0]
    parents = par_source.shape[0]
    qloc = qdir // n
    sources = low_index.shape[1]
    chains = 4

    low_rows = jnp.transpose(low_table.reshape(2, -1, kdir // 128, 128), (1, 2, 0, 3)).reshape(-1, 128)
    par_rows = jnp.transpose(par_table.reshape(2, -1, qdir // 128, 128), (1, 2, 0, 3)).reshape(-1, 128)

    pitches = (kdir + 8, 2 * boxes + 8, qloc + 8, 2 * parents + 8)
    kpitch, bpitch, qpitch, ppitch = pitches
    vmem = pl.BlockSpec(memory_space=pltpu.VMEM)
    smem = pl.BlockSpec(memory_space=pltpu.SMEM)
    stages = n.bit_length() - 1
    dma = pltpu.SemaphoreType.DMA
    return pl.pallas_call(
        functools.partial(kernel, n, listed, chains, pitches),
        out_shape=jax.ShapeDtypeStruct((2 * boxes * kdir, illums), F32),
        in_specs=[smem] + [vmem] * 10,
        out_specs=vmem,
        scratch_shapes=[
            pltpu.VMEM(low_rows.shape, F32),
            pltpu.VMEM(par_rows.shape, F32),
            pltpu.VMEM((qdir, 16), F32),
            pltpu.VMEM((kdir * bpitch, 2 * sources + -2 * sources % 128), F32),
            pltpu.VMEM((qloc * ppitch, 2 * parents), F32),
            pltpu.VMEM((2 * groups8, qdir, illums), BF16),
            pltpu.VMEM((n, 2 * groups8, qloc, illums), BF16),
            pltpu.VMEM((2 * parents * qpitch, illums), F32),
            pltpu.VMEM((2 * parents * qpitch, illums), F32),
            pltpu.VMEM((2, parents, qloc, illums), BF16),
            pltpu.VMEM((groups8, 2, 1, qdir, illums), BF16),
            pltpu.VMEM((kdir, 2 * boxes, illums), BF16),
            [pltpu.VMEM((kdir // 2 // chains, 2 * boxes, illums), BF16) for _ in range(chains)],
            pltpu.VMEM((kdir, 16 * listed, illums), BF16),
            pltpu.VMEM((kdir // 2, 16 * listed, illums), BF16),
            pltpu.VMEM((kdir, 16 * listed, illums), BF16),
            pltpu.VMEM((2 * boxes * kpitch, illums), F32),
            pltpu.VMEM((2 * boxes * kpitch, illums), F32),
            dma((groups8,)),
            dma((groups8,)),
            dma((groups8,)),
            dma((groups8,)),
            dma((chains,)),
            dma((chains,)),
            dma((chains, stages - 1)),
            dma((chains, stages - 1)),
            dma((chains, stages - 1)),
            dma((chains, stages - 1)),
        ],
        compiler_params=pltpu.CompilerParams(
            collective_id=0, has_side_effects=True, vmem_limit_bytes=56 * 1024 * 1024
        ),
    )(
        owner_block,
        patterns,
        low_index,
        low_mask,
        low_rows,
        par_source.T,
        par_index.T,
        par_mask.T,
        par_rows,
        interp,
        shift_angle,
    ).reshape(2, boxes, kdir, illums)


def solution(mesh):
    placed = (
        P(None, "box", None, "illum"),
        P(),
        P("box", None),
        P("box", None),
        P(),
        P(),
        P(),
        P(),
        P(),
        P(),
        P(),
    )
    return jax.shard_map(
        shards, mesh=mesh, in_specs=placed, out_specs=P(None, "box", None, "illum"), check_vma=False
    )
```
